32 devices in a mesh: ia: 4 (over y, core), ja: 2 (over x), ka: 4 (over z).
Axes of the slice: x: 2, y: 2, z: 4, core: 2. Of those that a mesh axis runs over, the one named last changes fastest.
Arguments:
- block_coords: int32 [4, 2, 4, 4, 3], P('ia', 'ja', 'ka'), may hold values from 0 to 3, as said below
- live_blocks: int32 [4, 2, 4], P('ia', 'ja', 'ka'), may hold values from 1 to 4, as said below
- counts: int32 [4, 2, 4, 4, 64, 4096], P('ia', 'ja', 'ka'), may hold values from 0 to 7
- factor_a: float32 [1024, 256], P(('ia', 'ja', 'ka')), may hold values from 0.3 to 9.6
- factor_b: float32 [512, 256], P(('ja', 'ka')), may hold values from 0.05 to 8
- factor_c: float32 [1024, 256], P('ka', 'ia'), may hold values from 0.05 to 8
Outputs:
- factor_new: float32 [1024, 256], P(('ia', 'ja', 'ka'))
The draws below stay inside these ranges and needn't reach their ends.
Inputs may be any that keep to these rules, and one draw needn't show every extreme that they name: `block_coords`: a device's slots name distinct blocks; slot 0 is always live, and every mode-1 block of the slab has a live block on some device. `live_blocks`: on some device all 4 slots are live.
All inputs are finite; a program needn't handle non-finite values.
Results may differ from the reference program's by a relative error of at most 0.00061.
Values may be sent and summed in bfloat16 or wider, within the bound.
A program may use at most 64 MiB of HBM per device.

```python
import math
import jax
import jax.numpy as jnp
from jax import lax

R = 256
BS = 64
RB1 = 4
RB2 = 4
RB3 = 4
SLOTS = 4
ROWS_I = 1024
ROWS_J = 512
ROWS_K = 1024
N_IA = 4
N_JA = 2
N_KA = 4


def draw_block_coords(key, part):
    total = N_IA * N_JA * N_KA
    many = RB1 * RB2 * RB3

    def single(index):
        sub = jax.random.fold_in(jax.random.fold_in(key, 11), index)
        first_key, other_key = jax.random.split(sub)
        group = index % (N_JA * N_KA) % RB1
        chosen = group * (RB2 * RB3) + jax.random.randint(first_key, (), 0, RB2 * RB3)
        positions = jnp.arange(many, dtype=jnp.int32)
        scores = jax.random.randint(other_key, (many,), 0, 2 ** 16) * many + positions
        scores = jnp.where(positions == chosen, 2 ** 30, scores)
        order = jnp.argsort(scores, stable=True).astype(jnp.int32)
        picked = jnp.concatenate([chosen[None].astype(jnp.int32), order[:SLOTS - 1]])
        return jnp.stack([picked // (RB2 * RB3), picked // RB3 % RB2, picked % RB3], axis=-1)
    result = jax.vmap(single)(jnp.arange(total, dtype=jnp.int32))
    return result.reshape(N_IA, N_JA, N_KA, SLOTS, 3).astype(jnp.int32)


def draw_live_blocks(key, part):
    total = N_IA * N_JA * N_KA
    key_base, key_busy, key_forced = jax.random.split(jax.random.fold_in(key, 23), 3)
    base = jax.random.randint(key_base, (total,), 1, max(2, SLOTS // 2 + 1))
    busy = jax.random.randint(key_busy, (total,), 0, 8) == 0
    forced = jax.random.randint(key_forced, (), 0, total)
    result = jnp.where(busy | (jnp.arange(total) == forced), SLOTS, base)
    return result.reshape(N_IA, N_JA, N_KA).astype(jnp.int32)


def topic_factor(key, seed_offset, row_count, lowest, highest, factor_boost):
    folded = jax.random.fold_in(key, seed_offset)
    key_level, key_marked = jax.random.split(folded)
    base_level = jnp.exp(jax.random.uniform(key_level, (row_count, R), jnp.float32, math.log(lowest), math.log(highest)))
    marked = jax.random.randint(key_marked, (row_count, R), 0, 32) == 0
    return jnp.where(marked, base_level * factor_boost, base_level).astype(jnp.float32)


def draw_factor_a(key, part):
    return topic_factor(key, 31, ROWS_I, 0.3, 1.2, 8.0)


def draw_factor_b(key, part):
    factor_boost = 30.0
    return topic_factor(key, 37, ROWS_J, 0.05, 0.2, factor_boost)


def draw_factor_c(key, part):
    factor_boost = 30.0
    return topic_factor(key, 41, ROWS_K, 0.05, 0.2, factor_boost)


def plant(values, own_key, low, top_value):
    index_at = [jax.random.randint(jax.random.fold_in(own_key, axis), (), 0, length) for axis, length in enumerate(values.shape)]
    widest = values.shape.index(max(values.shape))
    neighbour = index_at[:widest] + [(index_at[widest] + 1) % values.shape[widest]] + index_at[widest + 1:]
    return values.at[tuple(index_at)].set(low).at[tuple(neighbour)].set(top_value)


def setup_inputs(seed: int = 0) -> dict:
    streams_of = jax.random.split(jax.random.key(seed), 7)
    return {
        "block_coords": draw_block_coords(jax.random.fold_in(streams_of[6], 71), 0),
        "live_blocks": draw_live_blocks(jax.random.fold_in(streams_of[6], 71), 0),
        "counts": plant(jax.random.randint(streams_of[2], (N_IA, N_JA, N_KA, SLOTS, BS, BS * BS), 0, 8), jax.random.fold_in(streams_of[2], 1), 0, 7).astype(jnp.int32),
        "factor_a": draw_factor_a(jax.random.fold_in(streams_of[6], 71), 0),
        "factor_b": draw_factor_b(jax.random.fold_in(streams_of[6], 71), 0),
        "factor_c": draw_factor_c(jax.random.fold_in(streams_of[6], 71), 0),
    }


def reference(block_coords, live_blocks, counts, factor_a, factor_b, factor_c):
    devices_all = N_IA * N_JA * N_KA
    total = devices_all * SLOTS
    flat_coords = block_coords.reshape(total, 3)
    entry = jnp.arange(total, dtype=jnp.int32)
    device = entry // SLOTS
    slot = entry % SLOTS
    a_index = device // (N_JA * N_KA)
    b_index = (device // N_KA) % N_JA
    c_index = device % N_KA
    weight = (slot < live_blocks.reshape(devices_all)[device]).astype(jnp.float32)
    block_i = (a_index * RB1 + flat_coords[:, 0]).astype(jnp.int32)
    block_j = (b_index * RB2 + flat_coords[:, 1]).astype(jnp.int32)
    block_k = (c_index * RB3 + flat_coords[:, 2]).astype(jnp.int32)
    flat_counts = counts.reshape(total, BS, BS * BS)
    sums_b = factor_b.reshape(N_JA * RB2, BS, R).sum(axis=1)
    sums_c = factor_c.reshape(N_KA * RB3, BS, R).sum(axis=1)
    masses = sums_b[block_j] * sums_c[block_k] * weight[:, None]
    mass = jax.ops.segment_sum(masses, block_i, num_segments=N_IA * RB1)
    mass_rows = jnp.repeat(mass, BS, axis=0)

    def accumulate(factor):
        factor_low = factor.astype(jnp.bfloat16)

        def step(phi, item):
            gi, gj, gk, w, block_counts = item
            rows_b = lax.dynamic_slice_in_dim(factor_b, gj * BS, BS, 0)
            rows_c = lax.dynamic_slice_in_dim(factor_c, gk * BS, BS, 0)
            panel = (rows_b[:, None, :] * rows_c[None, :, :]).reshape(BS * BS, R).astype(jnp.bfloat16)
            block_a = lax.dynamic_slice_in_dim(factor_low, gi * BS, BS, 0)
            model = lax.dot_general(block_a, panel, (((1,), (1,)), ((), ())), preferred_element_type=jnp.float32)
            ratio = (block_counts.astype(jnp.float32) / model).astype(jnp.bfloat16)
            part = jnp.dot(ratio, panel, preferred_element_type=jnp.float32) * w
            old = lax.dynamic_slice_in_dim(phi, gi * BS, BS, 0)
            return lax.dynamic_update_slice_in_dim(phi, old + part, gi * BS, 0), None

        start = jnp.zeros((N_IA * RB1 * BS, R), jnp.float32)
        phi, _ = lax.scan(step, start, (block_i, block_j, block_k, weight, flat_counts))
        return phi

    first = factor_a * accumulate(factor_a) / mass_rows
    return first * accumulate(first) / mass_rows
```

```python
import functools

import jax
import jax.numpy as jnp
from jax import lax
from jax.experimental import pallas as pl
from jax.experimental.pallas import tpu as pltpu
from jax.sharding import PartitionSpec as P

RB1 = 4
RB2 = 4
RB3 = 4
MESH = pl.DeviceIdType.MESH


def loop(count, body, order=None):
    if count <= 8:
        for d in order or range(1, count):
            body(d)
    else:

        def step(d, carry):
            body(d)
            return carry

        lax.fori_loop(1, count, step, 0)


def pack(low, high):
    return jnp.bitwise_or(lax.shift_left(high, 16), low)


def unpack(words):
    return jnp.bitwise_and(words, 0xFFFF), lax.shift_right_logical(words, 16)


def scale_bits(rows):
    return max(1, 8 // rows)


def row_shift(shape):
    row = lax.broadcasted_iota(jnp.int32, shape, 0)
    return jnp.minimum(row * scale_bits(shape[0]), 31)


def encode(values):
    rows, rank = values.shape
    spare = scale_bits(rows)
    levels = 2 ** (16 - spare)
    top = jnp.maximum(jnp.max(values, axis=0, keepdims=True), 2.0 ** -100)
    exponent = jnp.floor(jnp.log2(top)) + 1.0
    level = (values * (levels * jnp.exp2(-exponent)) + 0.5).astype(jnp.int32)
    level = jnp.minimum(level, levels - 1)
    hidden = lax.shift_right_logical(
        jnp.broadcast_to(exponent.astype(jnp.int32) + 128, values.shape), row_shift(values.shape)
    )
    codes = lax.shift_left(level, spare) + jnp.bitwise_and(hidden, 2 ** spare - 1)
    return pack(codes[:, :rank // 2], codes[:, rank // 2:])


def decode(words):
    rows, half = words.shape
    spare = scale_bits(rows)
    found = []
    for codes in unpack(words):
        hidden = jnp.bitwise_and(codes, 2 ** spare - 1)[:8]
        exponent = jnp.sum(lax.shift_left(hidden, row_shift(hidden.shape)), axis=0, keepdims=True) - 128
        step = jnp.exp2(exponent.astype(jnp.float32)) * 2.0 ** (spare - 16)
        found.append(lax.shift_right_logical(codes, spare).astype(jnp.float32) * step)
    return jnp.concatenate(found, axis=1)


LOWEST, SPAN = 0.05 ** 0.5, 8.0 ** 0.5 - 0.05 ** 0.5


def encode_factor(values):
    half = values.shape[1] // 2
    level = ((jnp.sqrt(values) - LOWEST) * (65535 / SPAN) + 0.5).astype(jnp.int32)
    level = jnp.minimum(jnp.maximum(level, 0), 65535)
    return pack(level[:, :half], level[:, half:])


def decode_factor(words):
    roots = [codes.astype(jnp.float32) * (SPAN / 65535) + LOWEST for codes in unpack(words)]
    roots = jnp.concatenate(roots, axis=1)
    return roots * roots


def kernel(
    n_ia, n_ja, n_ka, bs,
    coords_in, live_in, counts, fa, fb, fc, out, coords, live,
    cnt, fbv, fcv, bpk, cpk, bg, cg, bfull, cfull, aown, alow, al, afull, panel, phi, ps, pr, ms, mr,
    local_sem, b_send, b_recv, c_send, c_recv, g_send, g_recv,
):
    n = n_ja * n_ka
    ia, ja, ka = lax.axis_index("ia"), lax.axis_index("ja"), lax.axis_index("ka")
    me = ja * n_ka + ka
    slots = cnt.shape[0]
    owned, rank = aown.shape
    rb = fb.shape[0]
    wc = fc.shape[0]

    far_first = sorted(range(1, n), key=lambda d: -min(d % n_ka, n_ka - d % n_ka))

    def group(d):
        t = lax.rem(me + d, n)
        return {"ja": lax.div(t, n_ka), "ka": lax.rem(t, n_ka)}

    def source(d):
        return lax.rem(me + n - d, n)

    load_a = pltpu.make_async_copy(fa, aown, local_sem.at[0])
    load_b = pltpu.make_async_copy(fb, fbv, local_sem.at[1])
    load_c = pltpu.make_async_copy(fc, fcv, local_sem.at[2])
    load_n = pltpu.make_async_copy(counts, cnt, local_sem.at[3])
    load_b.start()
    load_c.start()
    load_a.start()
    load_n.start()
    load_where = pltpu.make_async_copy(coords_in, coords, local_sem.at[4])
    load_live = pltpu.make_async_copy(live_in, live, local_sem.at[5])
    load_where.start()
    load_live.start()

    barrier = pltpu.get_barrier_semaphore()
    for axis, here, count in (("ka", ka, n_ka), ("ja", ja, n_ja), ("ia", ia, n_ia)):
        loop(
            count,
            lambda d: pl.semaphore_signal(
                barrier, inc=1, device_id={axis: lax.rem(here + d, count)}, device_id_type=MESH
            ),
        )
    load_a.wait()
    alow[0] = aown[...].astype(jnp.bfloat16)
    load_b.wait()
    bpk[...] = encode_factor(fbv[...])
    load_c.wait()
    cpk[...] = encode_factor(fcv[...])
    pl.semaphore_wait(barrier, n_ka + n_ja + n_ia - 3)

    halves = 2 if n_ia % 2 == 0 and rb % 16 == 0 else 1
    hb = rb // halves
    part = lax.rem(ia, halves)
    partner = ia + 1 - 2 * part

    def b_rows(whose, half):
        return bg.at[pl.ds(pl.multiple_of(whose * rb + half * hb, hb), hb)]

    def b_copy(d, whose):
        return pltpu.make_async_remote_copy(
            src_ref=bpk.at[pl.ds(pl.multiple_of(part * hb, hb), hb)], dst_ref=b_rows(whose, part),
            send_sem=b_send.at[0, d], recv_sem=b_recv.at[0, d],
            device_id={"ka": lax.rem(ka + d, n_ka)}, device_id_type=MESH,
        )

    def b_hand(d, half):
        rows = b_rows(lax.rem(ka + n_ka - d, n_ka), half)
        return pltpu.make_async_remote_copy(
            src_ref=rows, dst_ref=rows, send_sem=b_send.at[1, d], recv_sem=b_recv.at[1, d],
            device_id={"ia": partner}, device_id_type=MESH,
        )

    def c_copy(d, whose):
        ranks = pl.ds(pl.multiple_of(whose * wc, wc), wc)
        return pltpu.make_async_remote_copy(
            src_ref=cpk, dst_ref=cg.at[ranks], send_sem=c_send.at[d], recv_sem=c_recv.at[d],
            device_id={"ia": lax.rem(ia + d, n_ia)}, device_id_type=MESH,
        )

    def a_copy(d, whose):
        return pltpu.make_async_remote_copy(
            src_ref=alow.at[1], dst_ref=al.at[1, whose],
            send_sem=g_send.at[1, d], recv_sem=g_recv.at[1, d],
            device_id=group(d), device_id_type=MESH,
        )

    def a_across(d, whose):
        return pltpu.make_async_remote_copy(
            src_ref=alow.at[0], dst_ref=al.at[0, whose * n_ka + ka],
            send_sem=g_send.at[0, d * n_ka], recv_sem=g_recv.at[0, d * n_ka],
            device_id={"ja": lax.rem(ja + d, n_ja)}, device_id_type=MESH,
        )

    def a_along(e, d, whose):
        other = lax.rem(ja + n_ja - e, n_ja) * n_ka
        return pltpu.make_async_remote_copy(
            src_ref=alow.at[0] if isinstance(e, int) and e == 0 else al.at[0, other + ka],
            dst_ref=al.at[0, other + whose],
            send_sem=g_send.at[0, e * n_ka + d], recv_sem=g_recv.at[0, e * n_ka + d],
            device_id={"ka": lax.rem(ka + d, n_ka)}, device_id_type=MESH,
        )

    def phi_copy(turn, d, whose):
        return pltpu.make_async_remote_copy(
            src_ref=ps.at[lax.rem(me + d, n)], dst_ref=pr.at[turn, whose],
            send_sem=g_send.at[2 + turn, d], recv_sem=g_recv.at[2 + turn, d],
            device_id=group(d), device_id_type=MESH,
        )

    def mass_copy(d, whose):
        block = lax.div(lax.rem(me + d, n) * owned, bs)
        return pltpu.make_async_remote_copy(
            src_ref=ms.at[block], dst_ref=mr.at[whose],
            send_sem=g_send.at[4, d], recv_sem=g_recv.at[4, d],
            device_id=group(d), device_id_type=MESH,
        )

    loop(n_ka, lambda d: b_copy(d, ka).start())
    loop(n_ia, lambda d: c_copy(d, ia).start())
    loop(n_ja, lambda d: a_across(d, ja).start())
    loop(n_ka, lambda d: a_along(0, d, ka).start())
    al[0, me] = alow[0]

    phi[...] = jnp.zeros_like(phi)
    ms[...] = jnp.zeros_like(ms)
    bg[pl.ds(pl.multiple_of(ka * rb, rb), rb)] = bpk[...]
    cg[pl.ds(pl.multiple_of(ia * wc, wc), wc)] = cpk[...]
    load_where.wait()
    load_live.wait()


    def across(e):
        a_across(e, lax.rem(ja + n_ja - e, n_ja)).wait_recv()
        loop(n_ka, lambda d: a_along(e, d, ka).start())

    loop(n_ja, across)

    def hand_on(d):
        b_copy(d, lax.rem(ka + n_ka - d, n_ka)).wait_recv()
        if halves == 2:
            b_hand(d, part).start()

    loop(n_ka, hand_on)
    loop(n_ia, lambda d: c_copy(d, lax.rem(ia + n_ia - d, n_ia)).wait_recv())
    turned = decode_factor(cg[...]).T
    for q in range(cfull.shape[0]):
        cfull[q] = turned[q * bs:(q + 1) * bs]
    if halves == 2:
        loop(n_ka, lambda d: b_hand(d, 1 - part).wait_recv())
    for q in range(bfull.shape[0]):
        bfull[q] = decode_factor(bg[q * bs:(q + 1) * bs])

    def is_block(index, q):
        return jnp.full((bs, rank), index, jnp.int32) == q

    def live_weight(s):
        return jnp.minimum(jnp.maximum(live[0] - s, 0), 1).astype(jnp.float32)

    def piece(ref, index):
        return ref[index]

    def build(s, carry):
        rows_b = piece(bfull, coords[1, 0, s])
        rows_c = piece(cfull, coords[2, 0, s])
        mass = jnp.sum(rows_b, axis=0, keepdims=True) * jnp.sum(rows_c, axis=0, keepdims=True)
        mass = mass * live_weight(s)
        for q in range(RB1):
            ms[q] += jnp.where(is_block(coords[0, 0, s], q)[:1], mass, 0.0)
        return carry

    lax.fori_loop(0, slots, build, 0)
    mr[me] = ms[lax.div(me * owned, bs)]
    loop(n, lambda d: mass_copy(d, me).start())
    load_n.wait()

    def spread(turn):
        for q in range(RB1):
            each = bs // owned
            afull[q] = jnp.concatenate([al[turn, q * each + p] for p in range(each)])

    step_columns = min(1024, bs * bs)

    steps = [(s, first) for s in range(slots) for first in range(0, bs * bs, step_columns)]

    def accumulate(fresh):
        def model_of(item, block_a, rows_b, rows_c):
            s, first = item
            if fresh:
                rows = jnp.concatenate(
                    [
                        (rows_b[j:j + 1] * rows_c).astype(jnp.bfloat16)
                        for j in range(first // bs, (first + step_columns) // bs)
                    ]
                )
                panel[s, first:first + step_columns] = rows
            else:
                rows = panel[s, first:first + step_columns]
            model = lax.dot_general(
                block_a, rows, (((1,), (1,)), ((), ())), preferred_element_type=jnp.float32
            )
            return rows, model

        def start(item):
            s, first = item
            if first == 0:
                block_a = piece(afull, coords[0, 0, s])
                held[:] = [block_a, None, None]
                if fresh:
                    held[1:] = [piece(bfull, coords[1, 0, s]), piece(cfull, coords[2, 0, s])]
            return model_of(item, *held)

        held = []
        part = None
        ahead = start(steps[0])
        for at, (s, first) in enumerate(steps):
            rows, model = ahead
            if at + 1 < len(steps):
                ahead = start(steps[at + 1])
            here = cnt[s, :, first:first + step_columns].astype(jnp.float32)
            ratio = (here / model).astype(jnp.bfloat16)
            term = jnp.dot(ratio, rows, preferred_element_type=jnp.float32)
            part = term if first == 0 else part + term
            if first + step_columns == bs * bs:
                part = part * live_weight(s)
                for q in range(RB1):
                    phi[q * bs:(q + 1) * bs] += jnp.where(is_block(coords[0, 0, s], q), part, 0.0)

    def phi_rows(whose):
        return phi[pl.ds(pl.multiple_of(whose * owned, owned), owned)]

    def scattered(turn):
        def send(d):
            to = lax.rem(me + d, n)
            if owned % 8 == 0:
                ps[to] = encode(phi_rows(to))
            phi_copy(turn, d, me).start()

        if owned % 8:
            for p in range(n):
                ps[p] = encode(phi[p * owned:(p + 1) * owned])
        loop(n, send, far_first)
        if owned % 8:
            pr[turn, me] = ps[me]
            own = jnp.zeros((owned, rank), jnp.float32)
        else:
            pr[turn, me] = jnp.zeros_like(ps[me])
            own = phi_rows(me)
        loop(n, lambda d: phi_copy(turn, d, source(d)).wait_recv())
        total = own
        for p in range(n):
            part = decode(pr[turn, p])
            total += part
        return total

    for e in range(n_ja):
        loop(n_ka, lambda d: a_along(e, d, lax.rem(ka + n_ka - d, n_ka)).wait_recv())
    spread(0)
    accumulate(True)
    total = scattered(0)
    loop(n, lambda d: mass_copy(d, source(d)).wait_recv())
    mass = mr[0]
    for p in range(1, n):
        mass += mr[p]
    updated = aown[...] * total / mass
    alow[1] = updated.astype(jnp.bfloat16)
    loop(n, lambda d: a_copy(d, me).start(), far_first)
    phi[...] = jnp.zeros_like(phi)
    loop(n, lambda d: phi_copy(0, d, me).wait_send())
    aown[...] = updated
    al[1, me] = alow[1]
    loop(n, lambda d: a_copy(d, source(d)).wait_recv())
    spread(1)
    accumulate(False)
    total = scattered(1)
    out[...] = aown[...] * total / mass

    loop(n_ka, lambda d: b_copy(d, ka).wait_send())
    loop(n_ia, lambda d: c_copy(d, ia).wait_send())
    if halves == 2:
        loop(n_ka, lambda d: b_hand(d, part).wait_send())
    loop(n_ja, lambda d: a_across(d, ja).wait_send())
    for e in range(n_ja):
        loop(n_ka, lambda d: a_along(e, d, ka).wait_send())
    loop(n, lambda d: a_copy(d, me).wait_send())
    loop(n, lambda d: mass_copy(d, me).wait_send())
    loop(n, lambda d: phi_copy(1, d, me).wait_send())


def local(n_ia, n_ja, n_ka, block_coords, live_blocks, counts, factor_a, factor_b, factor_c):
    slots = block_coords.shape[-2]
    bs, cells = counts.shape[-2:]
    owned, rank = factor_a.shape
    rb = factor_b.shape[0]
    rc, wc = factor_c.shape
    n = n_ja * n_ka
    f32, bf16 = jnp.float32, jnp.bfloat16
    hbm = pl.BlockSpec(memory_space=pl.ANY)
    dma = pltpu.SemaphoreType.DMA
    return pl.pallas_call(
        functools.partial(kernel, n_ia, n_ja, n_ka, bs),
        out_shape=pltpu.VMEM((owned, rank), f32),
        in_specs=[hbm] * 6,
        out_specs=pl.BlockSpec(memory_space=pltpu.VMEM),
        scratch_shapes=[
            pltpu.SMEM((3, 1, slots), jnp.int32),
            pltpu.SMEM((1,), jnp.int32),
            pltpu.VMEM((slots, bs, cells), jnp.int32),
            pltpu.VMEM((rb, rank), f32),
            pltpu.VMEM((wc, rc), f32),
            pltpu.VMEM((rb, rank // 2), jnp.int32),
            pltpu.VMEM((wc, rc // 2), jnp.int32),
            pltpu.VMEM((n_ka * rb, rank // 2), jnp.int32),
            pltpu.VMEM((n_ia * wc, rc // 2), jnp.int32),
            pltpu.VMEM((n_ka * rb // bs, bs, rank), f32),
            pltpu.VMEM((rc // bs, bs, rank), f32),
            pltpu.VMEM((owned, rank), f32),
            pltpu.VMEM((2, owned, rank), bf16),
            pltpu.VMEM((2, n, owned, rank), bf16),
            pltpu.VMEM((RB1, bs, rank), bf16),
            pltpu.VMEM((slots, cells, rank), bf16),
            pltpu.VMEM((RB1 * bs, rank), f32),
            pltpu.VMEM((n, owned, rank // 2), jnp.int32),
            pltpu.VMEM((2, n, owned, rank // 2), jnp.int32),
            pltpu.VMEM((RB1, 1, rank), f32),
            pltpu.VMEM((n, 1, rank), f32),
            dma((6,)),
            dma((2, n_ka)),
            dma((2, n_ka)),
            dma((n_ia,)),
            dma((n_ia,)),
            dma((5, n)),
            dma((5, n)),
        ],
        compiler_params=pltpu.CompilerParams(
            collective_id=0, has_side_effects=True, vmem_limit_bytes=56 * 1024 * 1024
        ),
    )(
        jnp.swapaxes(block_coords, 3, 4).reshape(3, 1, slots), live_blocks.reshape(1),
        counts.reshape(slots, bs, cells), factor_a, factor_b, factor_c.T,
    )


def solution(mesh):
    placed = (
        P("ia", "ja", "ka", None, None),
        P("ia", "ja", "ka"),
        P("ia", "ja", "ka", None, None, None),
        P(("ia", "ja", "ka"), None),
        P(("ja", "ka"), None),
        P("ka", "ia"),
    )
    body = functools.partial(local, mesh.shape["ia"], mesh.shape["ja"], mesh.shape["ka"])
    return jax.shard_map(
        body, mesh=mesh, in_specs=placed, out_specs=P(("ia", "ja", "ka"), None), check_vma=False
    )
```

```python
import functools

import jax
import jax.numpy as jnp
from jax import lax
from jax.experimental import pallas as pl
from jax.experimental.pallas import tpu as pltpu
from jax.sharding import PartitionSpec as P

RB1 = 4
RB2 = 4
RB3 = 4
MESH = pl.DeviceIdType.MESH


def loop(count, body, order=None):
    if count <= 8:
        for d in order or range(1, count):
            body(d)
    else:

        def step(d, carry):
            body(d)
            return carry

        lax.fori_loop(1, count, step, 0)


def pack(low, high):
    return jnp.bitwise_or(lax.shift_left(high, 16), low)


def unpack(words):
    return jnp.bitwise_and(words, 0xFFFF), lax.shift_right_logical(words, 16)


def scale_bits(rows):
    return max(1, 8 // rows)


def row_shift(shape):
    row = lax.broadcasted_iota(jnp.int32, shape, 0)
    return jnp.minimum(row * scale_bits(shape[0]), 31)


def encode(values):
    rows, rank = values.shape
    spare = scale_bits(rows)
    levels = 2 ** (16 - spare)
    top = jnp.maximum(jnp.max(values, axis=0, keepdims=True), 2.0 ** -100)
    exponent = jnp.floor(jnp.log2(top)) + 1.0
    level = (values * (levels * jnp.exp2(-exponent)) + 0.5).astype(jnp.int32)
    level = jnp.minimum(level, levels - 1)
    hidden = lax.shift_right_logical(
        jnp.broadcast_to(exponent.astype(jnp.int32) + 128, values.shape), row_shift(values.shape)
    )
    codes = lax.shift_left(level, spare) + jnp.bitwise_and(hidden, 2 ** spare - 1)
    return pack(codes[:, :rank // 2], codes[:, rank // 2:])


def decode(words):
    rows, half = words.shape
    spare = scale_bits(rows)
    found = []
    for codes in unpack(words):
        hidden = jnp.bitwise_and(codes, 2 ** spare - 1)[:8]
        exponent = jnp.sum(lax.shift_left(hidden, row_shift(hidden.shape)), axis=0, keepdims=True) - 128
        step = jnp.exp2(exponent.astype(jnp.float32)) * 2.0 ** (spare - 16)
        found.append(lax.shift_right_logical(codes, spare).astype(jnp.float32) * step)
    return jnp.concatenate(found, axis=1)


LOWEST, SPAN = 0.05 ** 0.5, 8.0 ** 0.5 - 0.05 ** 0.5


def encode_factor(values):
    half = values.shape[1] // 2
    level = ((jnp.sqrt(values) - LOWEST) * (65535 / SPAN) + 0.5).astype(jnp.int32)
    level = jnp.minimum(jnp.maximum(level, 0), 65535)
    return pack(level[:, :half], level[:, half:])


def decode_factor(words):
    roots = [codes.astype(jnp.float32) * (SPAN / 65535) + LOWEST for codes in unpack(words)]
    roots = jnp.concatenate(roots, axis=1)
    return roots * roots


def kernel(
    n_ia, n_ja, n_ka, bs,
    coords_in, live_in, counts, fa, fb, fc, out, coords, live,
    cnt, fbv, fcv, bpk, cpk, bg, cg, bfull, cfull, aown, alow, al, afull, panel, turned_panel, phi, ps, pr, ms, mr,
    local_sem, b_send, b_recv, c_send, c_recv, g_send, g_recv,
):
    n = n_ja * n_ka
    ia, ja, ka = lax.axis_index("ia"), lax.axis_index("ja"), lax.axis_index("ka")
    me = ja * n_ka + ka
    slots = cnt.shape[0]
    owned, rank = aown.shape
    rb = fb.shape[0]
    wc = fc.shape[0]

    far_first = sorted(range(1, n), key=lambda d: -min(d % n_ka, n_ka - d % n_ka))

    def group(d):
        t = lax.rem(me + d, n)
        return {"ja": lax.div(t, n_ka), "ka": lax.rem(t, n_ka)}

    def source(d):
        return lax.rem(me + n - d, n)

    load_a = pltpu.make_async_copy(fa, aown, local_sem.at[0])
    load_b = pltpu.make_async_copy(fb, fbv, local_sem.at[1])
    load_c = pltpu.make_async_copy(fc, fcv, local_sem.at[2])
    load_n = pltpu.make_async_copy(counts, cnt, local_sem.at[3])
    load_b.start()
    load_c.start()
    load_a.start()
    load_n.start()
    load_where = pltpu.make_async_copy(coords_in, coords, local_sem.at[4])
    load_live = pltpu.make_async_copy(live_in, live, local_sem.at[5])
    load_where.start()
    load_live.start()

    barrier = pltpu.get_barrier_semaphore()
    for axis, here, count in (("ka", ka, n_ka), ("ja", ja, n_ja), ("ia", ia, n_ia)):
        loop(
            count,
            lambda d: pl.semaphore_signal(
                barrier, inc=1, device_id={axis: lax.rem(here + d, count)}, device_id_type=MESH
            ),
        )
    load_a.wait()
    alow[0] = aown[...].astype(jnp.bfloat16)
    load_b.wait()
    bpk[...] = encode_factor(fbv[...])
    load_c.wait()
    cpk[...] = encode_factor(fcv[...])
    pl.semaphore_wait(barrier, n_ka + n_ja + n_ia - 3)

    halves = 2 if n_ia % 2 == 0 and rb % 16 == 0 else 1
    hb = rb // halves
    part = lax.rem(ia, halves)
    partner = ia + 1 - 2 * part

    def b_rows(whose, half):
        return bg.at[pl.ds(pl.multiple_of(whose * rb + half * hb, hb), hb)]

    def b_copy(d, whose):
        return pltpu.make_async_remote_copy(
            src_ref=bpk.at[pl.ds(pl.multiple_of(part * hb, hb), hb)], dst_ref=b_rows(whose, part),
            send_sem=b_send.at[0, d], recv_sem=b_recv.at[0, d],
            device_id={"ka": lax.rem(ka + d, n_ka)}, device_id_type=MESH,
        )

    def b_hand(d, half):
        rows = b_rows(lax.rem(ka + n_ka - d, n_ka), half)
        return pltpu.make_async_remote_copy(
            src_ref=rows, dst_ref=rows, send_sem=b_send.at[1, d], recv_sem=b_recv.at[1, d],
            device_id={"ia": partner}, device_id_type=MESH,
        )

    def c_copy(d, whose):
        ranks = pl.ds(pl.multiple_of(whose * wc, wc), wc)
        return pltpu.make_async_remote_copy(
            src_ref=cpk, dst_ref=cg.at[ranks], send_sem=c_send.at[d], recv_sem=c_recv.at[d],
            device_id={"ia": lax.rem(ia + d, n_ia)}, device_id_type=MESH,
        )

    def a_copy(d, whose):
        return pltpu.make_async_remote_copy(
            src_ref=alow.at[1], dst_ref=al.at[1, whose],
            send_sem=g_send.at[1, d], recv_sem=g_recv.at[1, d],
            device_id=group(d), device_id_type=MESH,
        )

    def a_across(d, whose):
        return pltpu.make_async_remote_copy(
            src_ref=alow.at[0], dst_ref=al.at[0, whose * n_ka + ka],
            send_sem=g_send.at[0, d * n_ka], recv_sem=g_recv.at[0, d * n_ka],
            device_id={"ja": lax.rem(ja + d, n_ja)}, device_id_type=MESH,
        )

    def a_along(e, d, whose):
        other = lax.rem(ja + n_ja - e, n_ja) * n_ka
        return pltpu.make_async_remote_copy(
            src_ref=alow.at[0] if isinstance(e, int) and e == 0 else al.at[0, other + ka],
            dst_ref=al.at[0, other + whose],
            send_sem=g_send.at[0, e * n_ka + d], recv_sem=g_recv.at[0, e * n_ka + d],
            device_id={"ka": lax.rem(ka + d, n_ka)}, device_id_type=MESH,
        )

    def phi_copy(turn, d, whose):
        return pltpu.make_async_remote_copy(
            src_ref=ps.at[lax.rem(me + d, n)], dst_ref=pr.at[turn, whose],
            send_sem=g_send.at[2 + turn, d], recv_sem=g_recv.at[2 + turn, d],
            device_id=group(d), device_id_type=MESH,
        )

    def mass_copy(d, whose):
        block = lax.div(lax.rem(me + d, n) * owned, bs)
        return pltpu.make_async_remote_copy(
            src_ref=ms.at[block], dst_ref=mr.at[whose],
            send_sem=g_send.at[4, d], recv_sem=g_recv.at[4, d],
            device_id=group(d), device_id_type=MESH,
        )

    loop(n_ka, lambda d: b_copy(d, ka).start())
    loop(n_ia, lambda d: c_copy(d, ia).start())
    loop(n_ja, lambda d: a_across(d, ja).start())
    loop(n_ka, lambda d: a_along(0, d, ka).start())
    al[0, me] = alow[0]

    phi[...] = jnp.zeros_like(phi)
    ms[...] = jnp.zeros_like(ms)
    bg[pl.ds(pl.multiple_of(ka * rb, rb), rb)] = bpk[...]
    cg[pl.ds(pl.multiple_of(ia * wc, wc), wc)] = cpk[...]
    load_where.wait()
    load_live.wait()


    def across(e):
        a_across(e, lax.rem(ja + n_ja - e, n_ja)).wait_recv()
        loop(n_ka, lambda d: a_along(e, d, ka).start())

    loop(n_ja, across)

    def hand_on(d):
        b_copy(d, lax.rem(ka + n_ka - d, n_ka)).wait_recv()
        if halves == 2:
            b_hand(d, part).start()

    loop(n_ka, hand_on)
    loop(n_ia, lambda d: c_copy(d, lax.rem(ia + n_ia - d, n_ia)).wait_recv())
    turned = decode_factor(cg[...]).T
    for q in range(cfull.shape[0]):
        cfull[q] = turned[q * bs:(q + 1) * bs]
    if halves == 2:
        loop(n_ka, lambda d: b_hand(d, 1 - part).wait_recv())
    for q in range(bfull.shape[0]):
        bfull[q] = decode_factor(bg[q * bs:(q + 1) * bs])

    def is_block(index, q):
        return jnp.full((bs, rank), index, jnp.int32) == q

    def live_weight(s):
        return jnp.minimum(jnp.maximum(live[0] - s, 0), 1).astype(jnp.float32)

    def piece(ref, index):
        return ref[index]

    def build(s, carry):
        rows_b = piece(bfull, coords[1, 0, s])
        rows_c = piece(cfull, coords[2, 0, s])
        mass = jnp.sum(rows_b, axis=0, keepdims=True) * jnp.sum(rows_c, axis=0, keepdims=True)
        mass = mass * live_weight(s)
        for q in range(RB1):
            ms[q] += jnp.where(is_block(coords[0, 0, s], q)[:1], mass, 0.0)
        return carry

    lax.fori_loop(0, slots, build, 0)
    mr[me] = ms[lax.div(me * owned, bs)]
    loop(n, lambda d: mass_copy(d, me).start())
    load_n.wait()

    def spread(turn):
        for q in range(RB1):
            each = bs // owned
            afull[q] = jnp.concatenate([al[turn, q * each + p] for p in range(each)])

    step_columns = min(512, bs * bs)

    steps = [(s, first) for s in range(slots) for first in range(0, bs * bs, step_columns)]

    def accumulate(fresh):
        def model_of(item, block_a, rows_b, rows_c):
            s, first = item
            if fresh:
                rows = jnp.concatenate(
                    [
                        (rows_b[j:j + 1] * rows_c).astype(jnp.bfloat16)
                        for j in range(first // bs, (first + step_columns) // bs)
                    ]
                )
                columns = rows.T
                panel[s, first:first + step_columns] = rows
                turned_panel[s, :, first:first + step_columns] = columns
            else:
                rows = panel[s, first:first + step_columns]
                columns = turned_panel[s, :, first:first + step_columns]
            model = jnp.dot(block_a, columns, preferred_element_type=jnp.float32)
            return rows, model

        def start(item):
            s, first = item
            if first == 0:
                block_a = piece(afull, coords[0, 0, s])
                held[:] = [block_a, None, None]
                if fresh:
                    held[1:] = [piece(bfull, coords[1, 0, s]), piece(cfull, coords[2, 0, s])]
            return model_of(item, *held)

        held = []
        part = None
        ahead = start(steps[0])
        for at, (s, first) in enumerate(steps):
            rows, model = ahead
            if at + 1 < len(steps):
                ahead = start(steps[at + 1])
            here = cnt[s, :, first:first + step_columns].astype(jnp.float32)
            ratio = (here / model).astype(jnp.bfloat16)
            term = jnp.dot(ratio, rows, preferred_element_type=jnp.float32)
            part = term if first == 0 else part + term
            if first + step_columns == bs * bs:
                part = part * live_weight(s)
                for q in range(RB1):
                    phi[q * bs:(q + 1) * bs] += jnp.where(is_block(coords[0, 0, s], q), part, 0.0)

    def phi_rows(whose):
        return phi[pl.ds(pl.multiple_of(whose * owned, owned), owned)]

    def scattered(turn):
        def send(d):
            to = lax.rem(me + d, n)
            if owned % 8 == 0:
                ps[to] = encode(phi_rows(to))
            phi_copy(turn, d, me).start()

        if owned % 8:
            for p in range(n):
                ps[p] = encode(phi[p * owned:(p + 1) * owned])
        loop(n, send, far_first)
        if owned % 8:
            pr[turn, me] = ps[me]
            own = jnp.zeros((owned, rank), jnp.float32)
        else:
            pr[turn, me] = jnp.zeros_like(ps[me])
            own = phi_rows(me)
        loop(n, lambda d: phi_copy(turn, d, source(d)).wait_recv())
        total = own
        for p in range(n):
            part = decode(pr[turn, p])
            total += part
        return total

    for e in range(n_ja):
        loop(n_ka, lambda d: a_along(e, d, lax.rem(ka + n_ka - d, n_ka)).wait_recv())
    spread(0)
    accumulate(True)
    total = scattered(0)
    loop(n, lambda d: mass_copy(d, source(d)).wait_recv())
    mass = mr[0]
    for p in range(1, n):
        mass += mr[p]
    updated = aown[...] * total / mass
    alow[1] = updated.astype(jnp.bfloat16)
    loop(n, lambda d: a_copy(d, me).start(), far_first)
    phi[...] = jnp.zeros_like(phi)
    loop(n, lambda d: phi_copy(0, d, me).wait_send())
    aown[...] = updated
    al[1, me] = alow[1]
    loop(n, lambda d: a_copy(d, source(d)).wait_recv())
    spread(1)
    accumulate(False)
    total = scattered(1)
    out[...] = aown[...] * total / mass

    loop(n_ka, lambda d: b_copy(d, ka).wait_send())
    loop(n_ia, lambda d: c_copy(d, ia).wait_send())
    if halves == 2:
        loop(n_ka, lambda d: b_hand(d, part).wait_send())
    loop(n_ja, lambda d: a_across(d, ja).wait_send())
    for e in range(n_ja):
        loop(n_ka, lambda d: a_along(e, d, ka).wait_send())
    loop(n, lambda d: a_copy(d, me).wait_send())
    loop(n, lambda d: mass_copy(d, me).wait_send())
    loop(n, lambda d: phi_copy(1, d, me).wait_send())


def local(n_ia, n_ja, n_ka, block_coords, live_blocks, counts, factor_a, factor_b, factor_c):
    slots = block_coords.shape[-2]
    bs, cells = counts.shape[-2:]
    owned, rank = factor_a.shape
    rb = factor_b.shape[0]
    rc, wc = factor_c.shape
    n = n_ja * n_ka
    f32, bf16 = jnp.float32, jnp.bfloat16
    hbm = pl.BlockSpec(memory_space=pl.ANY)
    dma = pltpu.SemaphoreType.DMA
    return pl.pallas_call(
        functools.partial(kernel, n_ia, n_ja, n_ka, bs),
        out_shape=pltpu.VMEM((owned, rank), f32),
        in_specs=[hbm] * 6,
        out_specs=pl.BlockSpec(memory_space=pltpu.VMEM),
        scratch_shapes=[
            pltpu.SMEM((3, 1, slots), jnp.int32),
            pltpu.SMEM((1,), jnp.int32),
            pltpu.VMEM((slots, bs, cells), jnp.int32),
            pltpu.VMEM((rb, rank), f32),
            pltpu.VMEM((wc, rc), f32),
            pltpu.VMEM((rb, rank // 2), jnp.int32),
            pltpu.VMEM((wc, rc // 2), jnp.int32),
            pltpu.VMEM((n_ka * rb, rank // 2), jnp.int32),
            pltpu.VMEM((n_ia * wc, rc // 2), jnp.int32),
            pltpu.VMEM((n_ka * rb // bs, bs, rank), f32),
            pltpu.VMEM((rc // bs, bs, rank), f32),
            pltpu.VMEM((owned, rank), f32),
            pltpu.VMEM((2, owned, rank), bf16),
            pltpu.VMEM((2, n, owned, rank), bf16),
            pltpu.VMEM((RB1, bs, rank), bf16),
            pltpu.VMEM((slots, cells, rank), bf16),
            pltpu.VMEM((slots, rank, cells), bf16),
            pltpu.VMEM((RB1 * bs, rank), f32),
            pltpu.VMEM((n, owned, rank // 2), jnp.int32),
            pltpu.VMEM((2, n, owned, rank // 2), jnp.int32),
            pltpu.VMEM((RB1, 1, rank), f32),
            pltpu.VMEM((n, 1, rank), f32),
            dma((6,)),
            dma((2, n_ka)),
            dma((2, n_ka)),
            dma((n_ia,)),
            dma((n_ia,)),
            dma((5, n)),
            dma((5, n)),
        ],
        compiler_params=pltpu.CompilerParams(
            collective_id=0, has_side_effects=True, vmem_limit_bytes=56 * 1024 * 1024
        ),
    )(
        jnp.swapaxes(block_coords, 3, 4).reshape(3, 1, slots), live_blocks.reshape(1),
        counts.reshape(slots, bs, cells), factor_a, factor_b, factor_c.T,
    )


def solution(mesh):
    placed = (
        P("ia", "ja", "ka", None, None),
        P("ia", "ja", "ka"),
        P("ia", "ja", "ka", None, None, None),
        P(("ia", "ja", "ka"), None),
        P(("ja", "ka"), None),
        P("ka", "ia"),
    )
    body = functools.partial(local, mesh.shape["ia"], mesh.shape["ja"], mesh.shape["ka"])
    return jax.shard_map(
        body, mesh=mesh, in_specs=placed, out_specs=P(("ia", "ja", "ka"), None), check_vma=False
    )
```

```python
import functools

import jax
import jax.numpy as jnp
from jax import lax
from jax.experimental import pallas as pl
from jax.experimental.pallas import tpu as pltpu
from jax.sharding import PartitionSpec as P

RB1 = 4
RB2 = 4
RB3 = 4
MESH = pl.DeviceIdType.MESH


def loop(count, body, order=None):
    if count <= 8:
        for d in order or range(1, count):
            body(d)
    else:

        def step(d, carry):
            body(d)
            return carry

        lax.fori_loop(1, count, step, 0)


def pack(low, high):
    return jnp.bitwise_or(lax.shift_left(high, 16), low)


def unpack(words):
    return jnp.bitwise_and(words, 0xFFFF), lax.shift_right_logical(words, 16)


def scale_bits(rows):
    return max(1, 8 // rows)


def row_shift(shape):
    row = lax.broadcasted_iota(jnp.int32, shape, 0)
    return jnp.minimum(row * scale_bits(shape[0]), 31)


def encode(values):
    rows, rank = values.shape
    spare = scale_bits(rows)
    levels = 2 ** (16 - spare)
    top = jnp.maximum(jnp.max(values, axis=0, keepdims=True), 2.0 ** -100)
    exponent = jnp.floor(jnp.log2(top)) + 1.0
    level = (values * (levels * jnp.exp2(-exponent)) + 0.5).astype(jnp.int32)
    level = jnp.minimum(level, levels - 1)
    hidden = lax.shift_right_logical(
        jnp.broadcast_to(exponent.astype(jnp.int32) + 128, values.shape), row_shift(values.shape)
    )
    codes = lax.shift_left(level, spare) + jnp.bitwise_and(hidden, 2 ** spare - 1)
    return pack(codes[:, :rank // 2], codes[:, rank // 2:])


def decode(words):
    rows, half = words.shape
    spare = scale_bits(rows)
    found = []
    for codes in unpack(words):
        hidden = jnp.bitwise_and(codes, 2 ** spare - 1)[:8]
        exponent = jnp.sum(lax.shift_left(hidden, row_shift(hidden.shape)), axis=0, keepdims=True) - 128
        step = jnp.exp2(exponent.astype(jnp.float32)) * 2.0 ** (spare - 16)
        found.append(lax.shift_right_logical(codes, spare).astype(jnp.float32) * step)
    return jnp.concatenate(found, axis=1)


LOWEST, SPAN = 0.05 ** 0.5, 8.0 ** 0.5 - 0.05 ** 0.5


def encode_factor(values):
    half = values.shape[1] // 2
    level = ((jnp.sqrt(values) - LOWEST) * (65535 / SPAN) + 0.5).astype(jnp.int32)
    level = jnp.minimum(jnp.maximum(level, 0), 65535)
    return pack(level[:, :half], level[:, half:])


def decode_factor(words):
    roots = [codes.astype(jnp.float32) * (SPAN / 65535) + LOWEST for codes in unpack(words)]
    roots = jnp.concatenate(roots, axis=1)
    return roots * roots


def kernel(
    n_ia, n_ja, n_ka, bs,
    coords_in, live_in, counts, fa, fb, fc, out, coords, live,
    cnt, fbv, fcv, bpk, cpk, bg, cg, bfull, cfull, aown, alow, al, afull, panel, turned_panel, phi, ps, pr, ms,
    local_sem, b_send, b_recv, c_send, c_recv, g_send, g_recv, ready,
):
    n = n_ja * n_ka
    ia, ja, ka = lax.axis_index("ia"), lax.axis_index("ja"), lax.axis_index("ka")
    me = ja * n_ka + ka
    slots = cnt.shape[0]
    owned, rank = aown.shape
    rb = fb.shape[0]
    wc = fc.shape[0]
    mass_scale = 2.0 ** 30 / (8.0 * bs * slots ** 0.5)

    def far_first():
        found = []
        for j in range(n_ka - 1):
            rising = jnp.where(j >= ka, j + 1, j)
            left = n_ka - 1 - j
            falling = jnp.where(left <= ka, left - 1, left)
            t = jnp.where(2 * ka < n_ka, falling, rising)
            for e in range(n_ja - 1, -1, -1):
                found.append(lax.rem(ja + e, n_ja) * n_ka + t)
        for e in range(1, n_ja):
            found.append(lax.rem(ja + e, n_ja) * n_ka + ka)
        return [lax.rem(t + n - me, n) for t in found]

    far_first = far_first() if n <= 8 else None

    def group(d):
        t = lax.rem(me + d, n)
        return {"ja": lax.div(t, n_ka), "ka": lax.rem(t, n_ka)}

    def source(d):
        return lax.rem(me + n - d, n)

    load_a = pltpu.make_async_copy(fa, aown, local_sem.at[0])
    load_b = pltpu.make_async_copy(fb, fbv, local_sem.at[1])
    load_c = pltpu.make_async_copy(fc, fcv, local_sem.at[2])
    load_n = pltpu.make_async_copy(counts, cnt, local_sem.at[3])
    load_b.start()
    load_c.start()
    load_a.start()
    load_n.start()
    load_where = pltpu.make_async_copy(coords_in, coords, local_sem.at[4])
    load_live = pltpu.make_async_copy(live_in, live, local_sem.at[5])
    load_where.start()
    load_live.start()

    barrier = pltpu.get_barrier_semaphore()
    place = ka * n_ja + ja

    def member(t):
        return {"ja": lax.rem(t, n_ja), "ka": lax.div(t, n_ja)}

    def greet(d):
        @pl.when(place + d < n)
        def _():
            pl.semaphore_signal(
                barrier, inc=1, device_id=member(place + d), device_id_type=MESH
            )

    def greet_ia(d):
        @pl.when(ia + d < n_ia)
        def _():
            pl.semaphore_signal(barrier, inc=1, device_id={"ia": ia + d}, device_id_type=MESH)

    def answer(d):
        @pl.when(place >= d)
        def _():
            pl.semaphore_signal(
                ready.at[0, d], inc=1, device_id=member(place - d), device_id_type=MESH
            )

    def answer_ia(d):
        @pl.when(ia >= d)
        def _():
            pl.semaphore_signal(
                ready.at[1, d], inc=1, device_id={"ia": ia - d}, device_id_type=MESH
            )

    loop(n, greet)
    loop(n_ia, greet_ia)

    @pl.when(place + ia > 0)
    def _():
        pl.semaphore_wait(barrier, place + ia)

    loop(n, answer)
    loop(n_ia, answer_ia)

    load_a.wait()
    alow[0] = aown[...].astype(jnp.bfloat16)
    load_b.wait()
    bpk[...] = encode_factor(fbv[...])
    load_c.wait()
    cpk[...] = encode_factor(fcv[...])

    paired = n_ia % 2 == 0
    odd = lax.rem(ia, 2)
    partner = ia + 1 - 2 * odd

    def when_carrier(act):
        if paired:
            pl.when(odd == 1)(act)
        else:
            act()

    def b_rows(whose):
        return bg.at[pl.ds(pl.multiple_of(whose * rb, rb), rb)]

    def b_copy(d, whose):
        return pltpu.make_async_remote_copy(
            src_ref=bpk, dst_ref=b_rows(whose),
            send_sem=b_send.at[0, d], recv_sem=b_recv.at[0, d],
            device_id={"ka": lax.rem(ka + d, n_ka)}, device_id_type=MESH,
        )

    def b_hand(d):
        rows = b_rows(lax.rem(ka + n_ka - d, n_ka))
        return pltpu.make_async_remote_copy(
            src_ref=rows, dst_ref=rows, send_sem=b_send.at[1, d], recv_sem=b_recv.at[1, d],
            device_id={"ia": partner}, device_id_type=MESH,
        )

    def c_copy(d, whose):
        ranks = pl.ds(pl.multiple_of(whose * wc, wc), wc)
        return pltpu.make_async_remote_copy(
            src_ref=cpk, dst_ref=cg.at[ranks], send_sem=c_send.at[d], recv_sem=c_recv.at[d],
            device_id={"ia": lax.rem(ia + d, n_ia)}, device_id_type=MESH,
        )

    def a_copy(d, whose):
        return pltpu.make_async_remote_copy(
            src_ref=alow.at[1], dst_ref=al.at[1, whose],
            send_sem=g_send.at[1, d], recv_sem=g_recv.at[1, d],
            device_id=group(d), device_id_type=MESH,
        )

    def a_first(d):
        return pltpu.make_async_remote_copy(
            src_ref=alow.at[0], dst_ref=al.at[0, me],
            send_sem=g_send.at[0, d], recv_sem=g_recv.at[0, d],
            device_id=member(lax.rem(place + d, n)), device_id_type=MESH,
        )

    def phi_copy(turn, d, whose):
        return pltpu.make_async_remote_copy(
            src_ref=ps.at[lax.rem(me + d, n)], dst_ref=pr.at[turn, whose],
            send_sem=g_send.at[2 + turn, d], recv_sem=g_recv.at[2 + turn, d],
            device_id=group(d), device_id_type=MESH,
        )

    def send_group(d):
        if n <= 8:
            if d % n_ja == 0:
                when_carrier(b_copy(d // n_ja, ka).start)
        else:

            @pl.when(lax.rem(d, n_ja) == 0)
            def _():
                when_carrier(b_copy(lax.div(d, n_ja), ka).start)

        a_first(d).start()

    def send_c(d):
        c_copy(d, ia).start()

    def to_earlier(here, count, send, d):
        @pl.when(here + d >= count)
        def _():
            send(d)

    def to_later(at, here, count, send, d):
        @pl.when(here + d < count)
        def _():
            pl.semaphore_wait(ready.at[at, d], 1)
            send(d)

    loop(n, lambda d: to_earlier(place, n, send_group, d))
    loop(n_ia, lambda d: to_earlier(ia, n_ia, send_c, d))
    loop(n_ia, lambda d: to_later(1, ia, n_ia, send_c, d))
    loop(n, lambda d: to_later(0, place, n, send_group, d))
    al[0, me] = alow[0]

    phi[...] = jnp.zeros_like(phi)
    bg[pl.ds(pl.multiple_of(ka * rb, rb), rb)] = bpk[...]
    cg[pl.ds(pl.multiple_of(ia * wc, wc), wc)] = cpk[...]
    load_where.wait()
    load_live.wait()


    def hand_on(d):
        b_copy(d, lax.rem(ka + n_ka - d, n_ka)).wait_recv()
        if paired:
            b_hand(d).start()

    when_carrier(lambda: loop(n_ka, hand_on))
    loop(n_ia, lambda d: c_copy(d, lax.rem(ia + n_ia - d, n_ia)).wait_recv())
    turned = decode_factor(cg[...]).T
    for q in range(cfull.shape[0]):
        cfull[q] = turned[q * bs:(q + 1) * bs]
    if paired:

        @pl.when(odd == 0)
        def _():
            loop(n_ka, lambda d: b_hand(d).wait_recv())

    for q in range(bfull.shape[0]):
        bfull[q] = decode_factor(bg[q * bs:(q + 1) * bs])

    def is_block(index, q):
        return jnp.full((bs, rank), index, jnp.int32) == q

    def live_weight(s):
        return jnp.minimum(jnp.maximum(live[0] - s, 0), 1).astype(jnp.float32)

    def piece(ref, index):
        return ref[index]

    def build(s):
        rows_b = piece(bfull, coords[1, 0, s])
        rows_c = piece(cfull, coords[2, 0, s])
        mass = jnp.sum(rows_b, axis=0, keepdims=True) * jnp.sum(rows_c, axis=0, keepdims=True)
        mass = mass * live_weight(s)
        for q in range(RB1):
            there = jnp.where(is_block(coords[0, 0, s], q)[:1], mass, 0.0)
            ms[q] = there if s == 0 else ms[q] + there

    load_n.wait()

    def spread(turn):
        for q in range(RB1):
            each = bs // owned
            afull[q] = jnp.concatenate([al[turn, q * each + p] for p in range(each)])

    step_columns = min(512, bs * bs)

    steps = [(s, first) for s in range(slots) for first in range(0, bs * bs, step_columns)]

    def accumulate(fresh):
        def model_of(item, block_a, rows_b, rows_c):
            s, first = item
            if fresh:
                rows = jnp.concatenate(
                    [
                        (rows_b[j:j + 1] * rows_c).astype(jnp.bfloat16)
                        for j in range(first // bs, (first + step_columns) // bs)
                    ]
                )
                columns = rows.T
                panel[s, first:first + step_columns] = rows
                turned_panel[s, :, first:first + step_columns] = columns
            else:
                rows = panel[s, first:first + step_columns]
                columns = turned_panel[s, :, first:first + step_columns]
            model = jnp.dot(block_a, columns, preferred_element_type=jnp.float32)
            return rows, model

        def start(item):
            s, first = item
            if first == 0:
                block_a = piece(afull, coords[0, 0, s])
                held[:] = [block_a, None, None]
                if fresh:
                    held[1:] = [piece(bfull, coords[1, 0, s]), piece(cfull, coords[2, 0, s])]
            return model_of(item, *held)

        held = []
        part = None
        ahead = start(steps[0])
        for at, (s, first) in enumerate(steps):
            rows, model = ahead
            if at + 1 < len(steps):
                ahead = start(steps[at + 1])
            here = cnt[s, :, first:first + step_columns].astype(jnp.float32)
            ratio = (here / model).astype(jnp.bfloat16)
            term = jnp.dot(ratio, rows, preferred_element_type=jnp.float32)
            part = term if first == 0 else part + term
            if first + step_columns == bs * bs:
                if fresh:
                    build(s)
                part = part * live_weight(s)
                for q in range(RB1):
                    phi[q * bs:(q + 1) * bs] += jnp.where(is_block(coords[0, 0, s], q), part, 0.0)

    def phi_rows(whose):
        return phi[pl.ds(pl.multiple_of(whose * owned, owned), owned)]

    def put_mass(to):
        level = (jnp.sqrt(ms[lax.div(to * owned, bs)]) * mass_scale + 0.5).astype(jnp.int32)
        ps[to, owned:owned + 1] = level[:, :rank // 2]
        ps[to, owned + 1:] = level[:, rank // 2:]

    def take_mass(p):
        level = jnp.concatenate([pr[0, p, owned:owned + 1], pr[0, p, owned + 1:]], axis=1)
        root = level.astype(jnp.float32) * (1.0 / mass_scale)
        return root * root

    def scattered(turn):
        def send(d):
            to = lax.rem(me + d, n)
            if owned % 8 == 0:
                ps[to, :owned] = encode(phi_rows(to))
            if turn == 0:
                put_mass(to)
            phi_copy(turn, d, me).start()

        if owned % 8:
            for p in range(n):
                ps[p, :owned] = encode(phi[p * owned:(p + 1) * owned])
        loop(n, send, far_first)
        mass = ms[lax.div(me * owned, bs)]
        if owned % 8:
            pr[turn, me, :owned] = ps[me, :owned]
            total = jnp.zeros((owned, rank), jnp.float32)
        else:
            pr[turn, me, :owned] = jnp.zeros((owned, rank // 2), jnp.int32)
            total = phi_rows(me)
        pr[turn, me, owned:] = jnp.zeros((2, rank // 2), jnp.int32)
        loop(n, lambda d: phi_copy(turn, d, source(d)).wait_recv())
        for p in range(n):
            total += decode(pr[turn, p, :owned])
            if turn == 0:
                mass += take_mass(p)
        return total, mass

    loop(n, lambda d: a_first(d).wait_recv())
    spread(0)
    accumulate(True)
    total, mass = scattered(0)
    updated = aown[...] * total / mass
    alow[1] = updated.astype(jnp.bfloat16)
    loop(n, lambda d: a_copy(d, me).start(), far_first)
    phi[...] = jnp.zeros_like(phi)
    loop(n, lambda d: phi_copy(0, d, me).wait_send())
    aown[...] = updated
    al[1, me] = alow[1]
    loop(n, lambda d: a_copy(d, source(d)).wait_recv())
    spread(1)
    accumulate(False)
    total, _ = scattered(1)
    out[...] = aown[...] * total / mass

    when_carrier(lambda: loop(n_ka, lambda d: b_copy(d, ka).wait_send()))
    loop(n_ia, lambda d: c_copy(d, ia).wait_send())
    if paired:
        when_carrier(lambda: loop(n_ka, lambda d: b_hand(d).wait_send()))
    loop(n, lambda d: a_first(d).wait_send())
    loop(n, lambda d: a_copy(d, me).wait_send())
    loop(n, lambda d: phi_copy(1, d, me).wait_send())


def local(n_ia, n_ja, n_ka, block_coords, live_blocks, counts, factor_a, factor_b, factor_c):
    slots = block_coords.shape[-2]
    bs, cells = counts.shape[-2:]
    owned, rank = factor_a.shape
    rb = factor_b.shape[0]
    rc, wc = factor_c.shape
    n = n_ja * n_ka
    f32, bf16 = jnp.float32, jnp.bfloat16
    hbm = pl.BlockSpec(memory_space=pl.ANY)
    dma = pltpu.SemaphoreType.DMA
    return pl.pallas_call(
        functools.partial(kernel, n_ia, n_ja, n_ka, bs),
        out_shape=pltpu.VMEM((owned, rank), f32),
        in_specs=[hbm] * 6,
        out_specs=pl.BlockSpec(memory_space=pltpu.VMEM),
        scratch_shapes=[
            pltpu.SMEM((3, 1, slots), jnp.int32),
            pltpu.SMEM((1,), jnp.int32),
            pltpu.VMEM((slots, bs, cells), jnp.int32),
            pltpu.VMEM((rb, rank), f32),
            pltpu.VMEM((wc, rc), f32),
            pltpu.VMEM((rb, rank // 2), jnp.int32),
            pltpu.VMEM((wc, rc // 2), jnp.int32),
            pltpu.VMEM((n_ka * rb, rank // 2), jnp.int32),
            pltpu.VMEM((n_ia * wc, rc // 2), jnp.int32),
            pltpu.VMEM((n_ka * rb // bs, bs, rank), f32),
            pltpu.VMEM((rc // bs, bs, rank), f32),
            pltpu.VMEM((owned, rank), f32),
            pltpu.VMEM((2, owned, rank), bf16),
            pltpu.VMEM((2, n, owned, rank), bf16),
            pltpu.VMEM((RB1, bs, rank), bf16),
            pltpu.VMEM((slots, cells, rank), bf16),
            pltpu.VMEM((slots, rank, cells), bf16),
            pltpu.VMEM((RB1 * bs, rank), f32),
            pltpu.VMEM((n, owned + 2, rank // 2), jnp.int32),
            pltpu.VMEM((2, n, owned + 2, rank // 2), jnp.int32),
            pltpu.VMEM((RB1, 1, rank), f32),
            dma((6,)),
            dma((2, n_ka)),
            dma((2, n_ka)),
            dma((n_ia,)),
            dma((n_ia,)),
            dma((5, n)),
            dma((5, n)),
            pltpu.SemaphoreType.REGULAR((2, max(n_ia, n))),
        ],
        compiler_params=pltpu.CompilerParams(
            collective_id=0, has_side_effects=True, vmem_limit_bytes=56 * 1024 * 1024
        ),
    )(
        jnp.swapaxes(block_coords, 3, 4).reshape(3, 1, slots), live_blocks.reshape(1),
        counts.reshape(slots, bs, cells), factor_a, factor_b, factor_c.T,
    )


def solution(mesh):
    placed = (
        P("ia", "ja", "ka", None, None),
        P("ia", "ja", "ka"),
        P("ia", "ja", "ka", None, None, None),
        P(("ia", "ja", "ka"), None),
        P(("ja", "ka"), None),
        P("ka", "ia"),
    )
    body = functools.partial(local, mesh.shape["ia"], mesh.shape["ja"], mesh.shape["ka"])
    return jax.shard_map(
        body, mesh=mesh, in_specs=placed, out_specs=P(("ia", "ja", "ka"), None), check_vma=False
    )
```

```python
import functools

import jax
import jax.numpy as jnp
from jax import lax
from jax.experimental import pallas as pl
from jax.experimental.pallas import tpu as pltpu
from jax.sharding import PartitionSpec as P

RB1 = 4
RB2 = 4
RB3 = 4
MESH = pl.DeviceIdType.MESH


def loop(count, body, order=None):
    if count <= 8:
        for d in order or range(1, count):
            body(d)
    else:

        def step(d, carry):
            body(d)
            return carry

        lax.fori_loop(1, count, step, 0)


def pack(low, high):
    return jnp.bitwise_or(lax.shift_left(high, 16), low)


def unpack(words):
    return jnp.bitwise_and(words, 0xFFFF), lax.shift_right_logical(words, 16)


def scale_bits(rows):
    return max(1, 8 // rows)


def row_shift(shape):
    row = lax.broadcasted_iota(jnp.int32, shape, 0)
    return jnp.minimum(row * scale_bits(shape[0]), 31)


def encode(values):
    rows, rank = values.shape
    spare = scale_bits(rows)
    levels = 2 ** (16 - spare)
    top = jnp.maximum(jnp.max(values, axis=0, keepdims=True), 2.0 ** -100)
    exponent = jnp.floor(jnp.log2(top)) + 1.0
    level = (values * (levels * jnp.exp2(-exponent)) + 0.5).astype(jnp.int32)
    level = jnp.minimum(level, levels - 1)
    hidden = lax.shift_right_logical(
        jnp.broadcast_to(exponent.astype(jnp.int32) + 128, values.shape), row_shift(values.shape)
    )
    codes = lax.shift_left(level, spare) + jnp.bitwise_and(hidden, 2 ** spare - 1)
    return pack(codes[:, :rank // 2], codes[:, rank // 2:])


def decode(words):
    rows, half = words.shape
    spare = scale_bits(rows)
    found = []
    for codes in unpack(words):
        hidden = jnp.bitwise_and(codes, 2 ** spare - 1)[:8]
        exponent = jnp.sum(lax.shift_left(hidden, row_shift(hidden.shape)), axis=0, keepdims=True) - 128
        step = jnp.exp2(exponent.astype(jnp.float32)) * 2.0 ** (spare - 16)
        found.append(lax.shift_right_logical(codes, spare).astype(jnp.float32) * step)
    return jnp.concatenate(found, axis=1)


LOWEST, SPAN = 0.05 ** 0.5, 8.0 ** 0.5 - 0.05 ** 0.5


def encode_factor(values):
    half = values.shape[1] // 2
    level = ((jnp.sqrt(values) - LOWEST) * (65535 / SPAN) + 0.5).astype(jnp.int32)
    level = jnp.minimum(jnp.maximum(level, 0), 65535)
    return pack(level[:, :half], level[:, half:])


def decode_factor(words):
    roots = [codes.astype(jnp.float32) * (SPAN / 65535) + LOWEST for codes in unpack(words)]
    roots = jnp.concatenate(roots, axis=1)
    return roots * roots


def kernel(
    n_ia, n_ja, n_ka, bs,
    coords_in, live_in, counts, fa, fb, fc, out, coords, live,
    cnt, fbv, fcv, bpk, cpk, bg, cg, bfull, cfull, aown, alow, al, afull, panel, turned_panel, phi, ps, pr, ms,
    local_sem, b_send, b_recv, c_send, c_recv, g_send, g_recv,
):
    n = n_ja * n_ka
    ia, ja, ka = lax.axis_index("ia"), lax.axis_index("ja"), lax.axis_index("ka")
    me = ja * n_ka + ka
    slots = cnt.shape[0]
    owned, rank = aown.shape
    rb = fb.shape[0]
    wc = fc.shape[0]
    mass_scale = 2.0 ** 30 / (8.0 * bs * slots ** 0.5)

    far_members = []
    if n <= 8:
        for j in range(n_ka - 1):
            rising = jnp.where(j >= ka, j + 1, j)
            left = n_ka - 1 - j
            falling = jnp.where(left <= ka, left - 1, left)
            t = jnp.where(2 * ka < n_ka, falling, rising)
            far_members += [(t, e) for e in range(n_ja - 1, -1, -1)]
        far_members += [(ka, e) for e in range(1, n_ja)]
    far_first = [
        lax.rem(lax.rem(ja + e, n_ja) * n_ka + t + n - me, n) for t, e in far_members
    ] or None

    def group(d):
        t = lax.rem(me + d, n)
        return {"ja": lax.div(t, n_ka), "ka": lax.rem(t, n_ka)}

    def source(d):
        return lax.rem(me + n - d, n)

    load_a = pltpu.make_async_copy(fa, aown, local_sem.at[0])
    load_b = pltpu.make_async_copy(fb, fbv, local_sem.at[1])
    load_c = pltpu.make_async_copy(fc, fcv, local_sem.at[2])
    load_n = pltpu.make_async_copy(counts, cnt, local_sem.at[3])
    load_b.start()
    load_c.start()
    load_a.start()
    load_n.start()
    load_where = pltpu.make_async_copy(coords_in, coords, local_sem.at[4])
    load_live = pltpu.make_async_copy(live_in, live, local_sem.at[5])
    load_where.start()
    load_live.start()

    barrier = pltpu.get_barrier_semaphore()
    place = ka * n_ja + ja

    def member(t):
        return {"ja": lax.rem(t, n_ja), "ka": lax.div(t, n_ja)}

    def greet(d):
        pl.semaphore_signal(
            barrier, inc=1, device_id=member(lax.rem(place + d, n)), device_id_type=MESH
        )

    def greet_ia(d):
        pl.semaphore_signal(
            barrier, inc=1, device_id={"ia": lax.rem(ia + d, n_ia)}, device_id_type=MESH
        )

    loop(n, greet)
    loop(n_ia, greet_ia)

    load_a.wait()
    alow[0] = aown[...].astype(jnp.bfloat16)
    load_b.wait()
    bpk[...] = encode_factor(fbv[...])
    load_c.wait()
    cpk[...] = encode_factor(fcv[...])
    pl.semaphore_wait(barrier, n + n_ia - 2)

    paired = n_ia % 2 == 0
    odd = lax.rem(ia, 2)
    partner = ia + 1 - 2 * odd

    def when_carrier(act):
        if paired:
            pl.when(odd == 1)(act)
        else:
            act()

    def b_rows(whose):
        return bg.at[pl.ds(pl.multiple_of(whose * rb, rb), rb)]

    def b_copy(d, whose):
        return pltpu.make_async_remote_copy(
            src_ref=bpk, dst_ref=b_rows(whose),
            send_sem=b_send.at[0, d], recv_sem=b_recv.at[0, d],
            device_id={"ka": lax.rem(ka + d, n_ka)}, device_id_type=MESH,
        )

    def b_hand(d):
        rows = b_rows(lax.rem(ka + n_ka - d, n_ka))
        return pltpu.make_async_remote_copy(
            src_ref=rows, dst_ref=rows, send_sem=b_send.at[1, d], recv_sem=b_recv.at[1, d],
            device_id={"ia": partner}, device_id_type=MESH,
        )

    def c_copy(d, whose):
        ranks = pl.ds(pl.multiple_of(whose * wc, wc), wc)
        return pltpu.make_async_remote_copy(
            src_ref=cpk, dst_ref=cg.at[ranks], send_sem=c_send.at[d], recv_sem=c_recv.at[d],
            device_id={"ia": lax.rem(ia + d, n_ia)}, device_id_type=MESH,
        )

    def a_copy(d, whose):
        return pltpu.make_async_remote_copy(
            src_ref=alow.at[1], dst_ref=al.at[1, whose],
            send_sem=g_send.at[1, d], recv_sem=g_recv.at[1, d],
            device_id=group(d), device_id_type=MESH,
        )

    def a_first(d):
        return pltpu.make_async_remote_copy(
            src_ref=alow.at[0], dst_ref=al.at[0, me],
            send_sem=g_send.at[0, d], recv_sem=g_recv.at[0, d],
            device_id=member(lax.rem(place + d, n)), device_id_type=MESH,
        )

    def phi_copy(turn, d, whose):
        return pltpu.make_async_remote_copy(
            src_ref=ps.at[lax.rem(me + d, n)], dst_ref=pr.at[turn, whose],
            send_sem=g_send.at[2 + turn, d], recv_sem=g_recv.at[2 + turn, d],
            device_id=group(d), device_id_type=MESH,
        )

    def send_group(d):
        @pl.when(lax.rem(d, n_ja) == 0)
        def _():
            when_carrier(b_copy(lax.div(d, n_ja), ka).start)

        a_first(d).start()

    if far_members:
        loop(n_ia, lambda d: c_copy(d, ia).start())
        for t, e in far_members:
            if e == 0:
                when_carrier(b_copy(lax.rem(t + n_ka - ka, n_ka), ka).start)
        for t, e in far_members:
            a_first(lax.rem(t * n_ja + lax.rem(ja + e, n_ja) + n - place, n)).start()
    else:
        loop(n_ia, lambda d: c_copy(d, ia).start())
        loop(n, send_group)
    al[0, me] = alow[0]

    phi[...] = jnp.zeros_like(phi)
    bg[pl.ds(pl.multiple_of(ka * rb, rb), rb)] = bpk[...]
    cg[pl.ds(pl.multiple_of(ia * wc, wc), wc)] = cpk[...]
    load_where.wait()
    load_live.wait()


    def hand_on(d):
        b_copy(d, lax.rem(ka + n_ka - d, n_ka)).wait_recv()
        if paired:
            b_hand(d).start()

    when_carrier(lambda: loop(n_ka, hand_on))
    loop(n_ia, lambda d: c_copy(d, lax.rem(ia + n_ia - d, n_ia)).wait_recv())
    turned = decode_factor(cg[...]).T
    for q in range(cfull.shape[0]):
        cfull[q] = turned[q * bs:(q + 1) * bs]
    if paired:

        @pl.when(odd == 0)
        def _():
            loop(n_ka, lambda d: b_hand(d).wait_recv())

    for q in range(bfull.shape[0]):
        bfull[q] = decode_factor(bg[q * bs:(q + 1) * bs])

    def is_block(index, q):
        return jnp.full((bs, rank), index, jnp.int32) == q

    def live_weight(s):
        return jnp.minimum(jnp.maximum(live[0] - s, 0), 1).astype(jnp.float32)

    def piece(ref, index):
        return ref[index]

    def build(s):
        rows_b = piece(bfull, coords[1, 0, s])
        rows_c = piece(cfull, coords[2, 0, s])
        mass = jnp.sum(rows_b, axis=0, keepdims=True) * jnp.sum(rows_c, axis=0, keepdims=True)
        mass = mass * live_weight(s)
        for q in range(RB1):
            there = jnp.where(is_block(coords[0, 0, s], q)[:1], mass, 0.0)
            ms[q] = there if s == 0 else ms[q] + there

    load_n.wait()

    def spread(turn):
        for q in range(RB1):
            each = bs // owned
            afull[q] = jnp.concatenate([al[turn, q * each + p] for p in range(each)])

    step_columns = min(512, bs * bs)

    steps = [(s, first) for s in range(slots) for first in range(0, bs * bs, step_columns)]

    def accumulate(fresh):
        def model_of(item, block_a, rows_b, rows_c):
            s, first = item
            if fresh:
                rows = jnp.concatenate(
                    [
                        (rows_b[j:j + 1] * rows_c).astype(jnp.bfloat16)
                        for j in range(first // bs, (first + step_columns) // bs)
                    ]
                )
                columns = rows.T
                panel[s, first:first + step_columns] = rows
                turned_panel[s, :, first:first + step_columns] = columns
            else:
                rows = panel[s, first:first + step_columns]
                columns = turned_panel[s, :, first:first + step_columns]
            model = jnp.dot(block_a, columns, preferred_element_type=jnp.float32)
            return rows, model

        def start(item):
            s, first = item
            if first == 0:
                block_a = piece(afull, coords[0, 0, s])
                held[:] = [block_a, None, None]
                if fresh:
                    held[1:] = [piece(bfull, coords[1, 0, s]), piece(cfull, coords[2, 0, s])]
            return model_of(item, *held)

        held = []
        part = None
        ahead = start(steps[0])
        for at, (s, first) in enumerate(steps):
            rows, model = ahead
            if at + 1 < len(steps):
                ahead = start(steps[at + 1])
            here = cnt[s, :, first:first + step_columns].astype(jnp.float32)
            ratio = (here / model).astype(jnp.bfloat16)
            term = jnp.dot(ratio, rows, preferred_element_type=jnp.float32)
            part = term if first == 0 else part + term
            if first + step_columns == bs * bs:
                if fresh:
                    build(s)
                part = part * live_weight(s)
                for q in range(RB1):
                    phi[q * bs:(q + 1) * bs] += jnp.where(is_block(coords[0, 0, s], q), part, 0.0)

    def phi_rows(whose):
        return phi[pl.ds(pl.multiple_of(whose * owned, owned), owned)]

    def put_mass(to):
        level = (jnp.sqrt(ms[lax.div(to * owned, bs)]) * mass_scale + 0.5).astype(jnp.int32)
        ps[to, owned:owned + 1] = level[:, :rank // 2]
        ps[to, owned + 1:] = level[:, rank // 2:]

    def take_mass(p):
        level = jnp.concatenate([pr[0, p, owned:owned + 1], pr[0, p, owned + 1:]], axis=1)
        root = level.astype(jnp.float32) * (1.0 / mass_scale)
        return root * root

    def scattered(turn):
        def send(d):
            to = lax.rem(me + d, n)
            if owned % 8 == 0:
                ps[to, :owned] = encode(phi_rows(to))
            if turn == 0:
                put_mass(to)
            phi_copy(turn, d, me).start()

        if owned % 8:
            for p in range(n):
                ps[p, :owned] = encode(phi[p * owned:(p + 1) * owned])
        loop(n, send, far_first)
        mass = ms[lax.div(me * owned, bs)]
        if owned % 8:
            pr[turn, me, :owned] = ps[me, :owned]
            total = jnp.zeros((owned, rank), jnp.float32)
        else:
            pr[turn, me, :owned] = jnp.zeros((owned, rank // 2), jnp.int32)
            total = phi_rows(me)
        pr[turn, me, owned:] = jnp.zeros((2, rank // 2), jnp.int32)
        loop(n, lambda d: phi_copy(turn, d, source(d)).wait_recv())
        for p in range(n):
            total += decode(pr[turn, p, :owned])
            if turn == 0:
                mass += take_mass(p)
        return total, mass

    loop(n, lambda d: a_first(d).wait_recv())
    spread(0)
    accumulate(True)
    total, mass = scattered(0)
    updated = aown[...] * total / mass
    alow[1] = updated.astype(jnp.bfloat16)
    loop(n, lambda d: a_copy(d, me).start(), far_first)
    phi[...] = jnp.zeros_like(phi)
    loop(n, lambda d: phi_copy(0, d, me).wait_send())
    aown[...] = updated
    al[1, me] = alow[1]
    loop(n, lambda d: a_copy(d, source(d)).wait_recv())
    spread(1)
    accumulate(False)
    total, _ = scattered(1)
    out[...] = aown[...] * total / mass

    when_carrier(lambda: loop(n_ka, lambda d: b_copy(d, ka).wait_send()))
    loop(n_ia, lambda d: c_copy(d, ia).wait_send())
    if paired:
        when_carrier(lambda: loop(n_ka, lambda d: b_hand(d).wait_send()))
    loop(n, lambda d: a_first(d).wait_send())
    loop(n, lambda d: a_copy(d, me).wait_send())
    loop(n, lambda d: phi_copy(1, d, me).wait_send())


def local(n_ia, n_ja, n_ka, block_coords, live_blocks, counts, factor_a, factor_b, factor_c):
    slots = block_coords.shape[-2]
    bs, cells = counts.shape[-2:]
    owned, rank = factor_a.shape
    rb = factor_b.shape[0]
    rc, wc = factor_c.shape
    n = n_ja * n_ka
    f32, bf16 = jnp.float32, jnp.bfloat16
    hbm = pl.BlockSpec(memory_space=pl.ANY)
    dma = pltpu.SemaphoreType.DMA
    return pl.pallas_call(
        functools.partial(kernel, n_ia, n_ja, n_ka, bs),
        out_shape=pltpu.VMEM((owned, rank), f32),
        in_specs=[hbm] * 6,
        out_specs=pl.BlockSpec(memory_space=pltpu.VMEM),
        scratch_shapes=[
            pltpu.SMEM((3, 1, slots), jnp.int32),
            pltpu.SMEM((1,), jnp.int32),
            pltpu.VMEM((slots, bs, cells), jnp.int32),
            pltpu.VMEM((rb, rank), f32),
            pltpu.VMEM((wc, rc), f32),
            pltpu.VMEM((rb, rank // 2), jnp.int32),
            pltpu.VMEM((wc, rc // 2), jnp.int32),
            pltpu.VMEM((n_ka * rb, rank // 2), jnp.int32),
            pltpu.VMEM((n_ia * wc, rc // 2), jnp.int32),
            pltpu.VMEM((n_ka * rb // bs, bs, rank), f32),
            pltpu.VMEM((rc // bs, bs, rank), f32),
            pltpu.VMEM((owned, rank), f32),
            pltpu.VMEM((2, owned, rank), bf16),
            pltpu.VMEM((2, n, owned, rank), bf16),
            pltpu.VMEM((RB1, bs, rank), bf16),
            pltpu.VMEM((slots, cells, rank), bf16),
            pltpu.VMEM((slots, rank, cells), bf16),
            pltpu.VMEM((RB1 * bs, rank), f32),
            pltpu.VMEM((n, owned + 2, rank // 2), jnp.int32),
            pltpu.VMEM((2, n, owned + 2, rank // 2), jnp.int32),
            pltpu.VMEM((RB1, 1, rank), f32),
            dma((6,)),
            dma((2, n_ka)),
            dma((2, n_ka)),
            dma((n_ia,)),
            dma((n_ia,)),
            dma((5, n)),
            dma((5, n)),
        ],
        compiler_params=pltpu.CompilerParams(
            collective_id=0, has_side_effects=True, vmem_limit_bytes=56 * 1024 * 1024
        ),
    )(
        jnp.swapaxes(block_coords, 3, 4).reshape(3, 1, slots), live_blocks.reshape(1),
        counts.reshape(slots, bs, cells), factor_a, factor_b, factor_c.T,
    )


def solution(mesh):
    placed = (
        P("ia", "ja", "ka", None, None),
        P("ia", "ja", "ka"),
        P("ia", "ja", "ka", None, None, None),
        P(("ia", "ja", "ka"), None),
        P(("ja", "ka"), None),
        P("ka", "ia"),
    )
    body = functools.partial(local, mesh.shape["ia"], mesh.shape["ja"], mesh.shape["ka"])
    return jax.shard_map(
        body, mesh=mesh, in_specs=placed, out_specs=P(("ia", "ja", "ka"), None), check_vma=False
    )
```

```python
import functools

import jax
import jax.numpy as jnp
from jax import lax
from jax.experimental import pallas as pl
from jax.experimental.pallas import tpu as pltpu
from jax.sharding import PartitionSpec as P

RB1 = 4
RB2 = 4
RB3 = 4
MESH = pl.DeviceIdType.MESH


def loop(count, body, order=None):
    if count <= 8:
        for d in order or range(1, count):
            body(d)
    else:

        def step(d, carry):
            body(d)
            return carry

        lax.fori_loop(1, count, step, 0)


def pack(low, high):
    return jnp.bitwise_or(lax.shift_left(high, 16), low)


def unpack(words):
    return jnp.bitwise_and(words, 0xFFFF), lax.shift_right_logical(words, 16)


def scale_bits(rows):
    return max(1, 8 // rows)


def row_shift(shape):
    row = lax.broadcasted_iota(jnp.int32, shape, 0)
    return jnp.minimum(row * scale_bits(shape[0]), 31)


def encode(values):
    rows, rank = values.shape
    spare = scale_bits(rows)
    levels = 2 ** (16 - spare)
    top = jnp.maximum(jnp.max(values, axis=0, keepdims=True), 2.0 ** -100)
    exponent = jnp.floor(jnp.log2(top)) + 1.0
    level = (values * (levels * jnp.exp2(-exponent)) + 0.5).astype(jnp.int32)
    level = jnp.minimum(level, levels - 1)
    hidden = lax.shift_right_logical(
        jnp.broadcast_to(exponent.astype(jnp.int32) + 128, values.shape), row_shift(values.shape)
    )
    codes = lax.shift_left(level, spare) + jnp.bitwise_and(hidden, 2 ** spare - 1)
    return pack(codes[:, :rank // 2], codes[:, rank // 2:])


def decode(words):
    rows, half = words.shape
    spare = scale_bits(rows)
    found = []
    for codes in unpack(words):
        hidden = jnp.bitwise_and(codes, 2 ** spare - 1)[:8]
        exponent = jnp.sum(lax.shift_left(hidden, row_shift(hidden.shape)), axis=0, keepdims=True) - 128
        step = jnp.exp2(exponent.astype(jnp.float32)) * 2.0 ** (spare - 16)
        found.append(lax.shift_right_logical(codes, spare).astype(jnp.float32) * step)
    return jnp.concatenate(found, axis=1)


LOWEST, SPAN = 0.05 ** 0.5, 8.0 ** 0.5 - 0.05 ** 0.5


def encode_factor(values):
    half = values.shape[1] // 2
    level = ((jnp.sqrt(values) - LOWEST) * (65535 / SPAN) + 0.5).astype(jnp.int32)
    level = jnp.minimum(jnp.maximum(level, 0), 65535)
    return pack(level[:, :half], level[:, half:])


def decode_factor(words):
    roots = [codes.astype(jnp.float32) * (SPAN / 65535) + LOWEST for codes in unpack(words)]
    roots = jnp.concatenate(roots, axis=1)
    return roots * roots


def kernel(
    n_ia, n_ja, n_ka, bs,
    coords_in, live_in, counts, fa, fb, fc, out, coords, live,
    cnt, fbv, fcv, bpk, cpk, bg, cg, bfull, cfull, aown, alow, al, afull, panel, turned_panel, phi, ps, pr, ms,
    local_sem, b_send, b_recv, c_send, c_recv, g_send, g_recv,
):
    n = n_ja * n_ka
    ia, ja, ka = lax.axis_index("ia"), lax.axis_index("ja"), lax.axis_index("ka")
    me = ja * n_ka + ka
    slots = cnt.shape[0]
    owned, rank = aown.shape
    rb = fb.shape[0]
    wc = fc.shape[0]
    mass_scale = 2.0 ** 30 / (8.0 * bs * slots ** 0.5)

    far_members = []
    if n <= 8:
        for j in range(n_ka - 1):
            rising = jnp.where(j >= ka, j + 1, j)
            left = n_ka - 1 - j
            falling = jnp.where(left <= ka, left - 1, left)
            t = jnp.where(2 * ka < n_ka, falling, rising)
            far_members += [(t, e) for e in range(n_ja - 1, -1, -1)]
        far_members += [(ka, e) for e in range(1, n_ja)]
        hops = [n_ka - 1 - at // n_ja + (e > 0) for at, (t, e) in enumerate(far_members)]
        ranked = sorted(range(len(hops)), key=lambda at: -hops[at])
        far_members = [far_members[at] for at in ranked]
    far_first = [
        lax.rem(lax.rem(ja + e, n_ja) * n_ka + t + n - me, n) for t, e in far_members
    ] or None

    def group(d):
        t = lax.rem(me + d, n)
        return {"ja": lax.div(t, n_ka), "ka": lax.rem(t, n_ka)}

    def source(d):
        return lax.rem(me + n - d, n)

    load_a = pltpu.make_async_copy(fa, aown, local_sem.at[0])
    load_b = pltpu.make_async_copy(fb, fbv, local_sem.at[1])
    load_c = pltpu.make_async_copy(fc, fcv, local_sem.at[2])
    load_n = pltpu.make_async_copy(counts, cnt, local_sem.at[3])
    load_b.start()
    load_c.start()
    load_a.start()
    load_n.start()
    load_where = pltpu.make_async_copy(coords_in, coords, local_sem.at[4])
    load_live = pltpu.make_async_copy(live_in, live, local_sem.at[5])
    load_where.start()
    load_live.start()

    barrier = pltpu.get_barrier_semaphore()
    place = ka * n_ja + ja

    def member(t):
        return {"ja": lax.rem(t, n_ja), "ka": lax.div(t, n_ja)}

    def greet(d):
        pl.semaphore_signal(
            barrier, inc=1, device_id=member(lax.rem(place + d, n)), device_id_type=MESH
        )

    def greet_ia(d):
        pl.semaphore_signal(
            barrier, inc=1, device_id={"ia": lax.rem(ia + d, n_ia)}, device_id_type=MESH
        )

    loop(n, greet)
    loop(n_ia, greet_ia)

    load_a.wait()
    alow[0] = aown[...].astype(jnp.bfloat16)
    load_b.wait()
    bpk[...] = encode_factor(fbv[...])
    load_c.wait()
    cpk[...] = encode_factor(fcv[...])
    pl.semaphore_wait(barrier, n + n_ia - 2)

    paired = n_ia % 2 == 0
    odd = lax.rem(ia, 2)
    partner = ia + 1 - 2 * odd

    def when_carrier(act):
        if paired:
            pl.when(odd == 1)(act)
        else:
            act()

    def b_rows(whose):
        return bg.at[pl.ds(pl.multiple_of(whose * rb, rb), rb)]

    def b_copy(d, whose):
        return pltpu.make_async_remote_copy(
            src_ref=bpk, dst_ref=b_rows(whose),
            send_sem=b_send.at[0, d], recv_sem=b_recv.at[0, d],
            device_id={"ka": lax.rem(ka + d, n_ka)}, device_id_type=MESH,
        )

    def b_hand(d):
        rows = b_rows(lax.rem(ka + n_ka - d, n_ka))
        return pltpu.make_async_remote_copy(
            src_ref=rows, dst_ref=rows, send_sem=b_send.at[1, d], recv_sem=b_recv.at[1, d],
            device_id={"ia": partner}, device_id_type=MESH,
        )

    def c_copy(d, whose):
        ranks = pl.ds(pl.multiple_of(whose * wc, wc), wc)
        return pltpu.make_async_remote_copy(
            src_ref=cpk, dst_ref=cg.at[ranks], send_sem=c_send.at[d], recv_sem=c_recv.at[d],
            device_id={"ia": lax.rem(ia + d, n_ia)}, device_id_type=MESH,
        )

    def a_copy(d, whose):
        return pltpu.make_async_remote_copy(
            src_ref=alow.at[1], dst_ref=al.at[1, whose],
            send_sem=g_send.at[1, d], recv_sem=g_recv.at[1, d],
            device_id=group(d), device_id_type=MESH,
        )

    def a_first(d):
        return pltpu.make_async_remote_copy(
            src_ref=alow.at[0], dst_ref=al.at[0, me],
            send_sem=g_send.at[0, d], recv_sem=g_recv.at[0, d],
            device_id=member(lax.rem(place + d, n)), device_id_type=MESH,
        )

    def phi_copy(turn, d, whose):
        return pltpu.make_async_remote_copy(
            src_ref=ps.at[lax.rem(me + d, n)], dst_ref=pr.at[turn, whose],
            send_sem=g_send.at[2 + turn, d], recv_sem=g_recv.at[2 + turn, d],
            device_id=group(d), device_id_type=MESH,
        )

    def send_group(d):
        @pl.when(lax.rem(d, n_ja) == 0)
        def _():
            when_carrier(b_copy(lax.div(d, n_ja), ka).start)

        a_first(d).start()

    if far_members:
        loop(n_ia, lambda d: c_copy(d, ia).start())
        for t, e in far_members:
            if e == 0:
                when_carrier(b_copy(lax.rem(t + n_ka - ka, n_ka), ka).start)
        for t, e in far_members:
            a_first(lax.rem(t * n_ja + lax.rem(ja + e, n_ja) + n - place, n)).start()
    else:
        loop(n_ia, lambda d: c_copy(d, ia).start())
        loop(n, send_group)
    al[0, me] = alow[0]

    phi[...] = jnp.zeros_like(phi)
    bg[pl.ds(pl.multiple_of(ka * rb, rb), rb)] = bpk[...]
    cg[pl.ds(pl.multiple_of(ia * wc, wc), wc)] = cpk[...]
    load_where.wait()
    load_live.wait()


    def hand_on(d):
        b_copy(d, lax.rem(ka + n_ka - d, n_ka)).wait_recv()
        if paired:
            b_hand(d).start()

    when_carrier(lambda: loop(n_ka, hand_on))
    loop(n_ia, lambda d: c_copy(d, lax.rem(ia + n_ia - d, n_ia)).wait_recv())
    turned = decode_factor(cg[...]).T
    for q in range(cfull.shape[0]):
        cfull[q] = turned[q * bs:(q + 1) * bs]
    if paired:

        @pl.when(odd == 0)
        def _():
            loop(n_ka, lambda d: b_hand(d).wait_recv())

    for q in range(bfull.shape[0]):
        bfull[q] = decode_factor(bg[q * bs:(q + 1) * bs])

    def is_block(index, q):
        return jnp.full((bs, rank), index, jnp.int32) == q

    def live_weight(s):
        return jnp.minimum(jnp.maximum(live[0] - s, 0), 1).astype(jnp.float32)

    def piece(ref, index):
        return ref[index]

    def build(s):
        rows_b = piece(bfull, coords[1, 0, s])
        rows_c = piece(cfull, coords[2, 0, s])
        mass = jnp.sum(rows_b, axis=0, keepdims=True) * jnp.sum(rows_c, axis=0, keepdims=True)
        mass = mass * live_weight(s)
        for q in range(RB1):
            there = jnp.where(is_block(coords[0, 0, s], q)[:1], mass, 0.0)
            ms[q] = there if s == 0 else ms[q] + there

    load_n.wait()

    def spread(turn):
        for q in range(RB1):
            each = bs // owned
            afull[q] = jnp.concatenate([al[turn, q * each + p] for p in range(each)])

    step_columns = min(256, bs * bs)

    steps = [(s, first) for s in range(slots) for first in range(0, bs * bs, step_columns)]

    def accumulate(fresh):
        def model_of(item, block_a, rows_b, rows_c):
            s, first = item
            if fresh:
                rows = jnp.concatenate(
                    [
                        (rows_b[j:j + 1] * rows_c).astype(jnp.bfloat16)
                        for j in range(first // bs, (first + step_columns) // bs)
                    ]
                )
                columns = rows.T
                panel[s, first:first + step_columns] = rows
                turned_panel[s, :, first:first + step_columns] = columns
            else:
                rows = panel[s, first:first + step_columns]
                columns = turned_panel[s, :, first:first + step_columns]
            model = jnp.dot(block_a, columns, preferred_element_type=jnp.float32)
            return rows, model

        def start(item):
            s, first = item
            if first == 0:
                block_a = piece(afull, coords[0, 0, s])
                held[:] = [block_a, None, None]
                if fresh:
                    held[1:] = [piece(bfull, coords[1, 0, s]), piece(cfull, coords[2, 0, s])]
            return model_of(item, *held)

        held = []
        part = None
        ahead = start(steps[0])
        for at, (s, first) in enumerate(steps):
            rows, model = ahead
            if at + 1 < len(steps):
                ahead = start(steps[at + 1])
            here = cnt[s, :, first:first + step_columns].astype(jnp.float32)
            ratio = (here / model).astype(jnp.bfloat16)
            term = jnp.dot(ratio, rows, preferred_element_type=jnp.float32)
            part = term if first == 0 else part + term
            if first + step_columns == bs * bs:
                if fresh:
                    build(s)
                part = part * live_weight(s)
                for q in range(RB1):
                    phi[q * bs:(q + 1) * bs] += jnp.where(is_block(coords[0, 0, s], q), part, 0.0)

    def phi_rows(whose):
        return phi[pl.ds(pl.multiple_of(whose * owned, owned), owned)]

    def put_mass(to):
        level = (jnp.sqrt(ms[lax.div(to * owned, bs)]) * mass_scale + 0.5).astype(jnp.int32)
        ps[to, owned:owned + 1] = level[:, :rank // 2]
        ps[to, owned + 1:] = level[:, rank // 2:]

    def take_mass(p):
        level = jnp.concatenate([pr[0, p, owned:owned + 1], pr[0, p, owned + 1:]], axis=1)
        root = level.astype(jnp.float32) * (1.0 / mass_scale)
        return root * root

    def scattered(turn):
        def send(d):
            to = lax.rem(me + d, n)
            if owned % 8 == 0:
                ps[to, :owned] = encode(phi_rows(to))
            if turn == 0:
                put_mass(to)
            phi_copy(turn, d, me).start()

        if owned % 8:
            for p in range(n):
                ps[p, :owned] = encode(phi[p * owned:(p + 1) * owned])
        loop(n, send, far_first)
        mass = ms[lax.div(me * owned, bs)]
        if owned % 8:
            pr[turn, me, :owned] = ps[me, :owned]
            total = jnp.zeros((owned, rank), jnp.float32)
        else:
            pr[turn, me, :owned] = jnp.zeros((owned, rank // 2), jnp.int32)
            total = phi_rows(me)
        pr[turn, me, owned:] = jnp.zeros((2, rank // 2), jnp.int32)
        loop(n, lambda d: phi_copy(turn, d, source(d)).wait_recv())
        for p in range(n):
            total += decode(pr[turn, p, :owned])
            if turn == 0:
                mass += take_mass(p)
        return total, mass

    loop(n, lambda d: a_first(d).wait_recv())
    spread(0)
    accumulate(True)
    total, mass = scattered(0)
    updated = aown[...] * total / mass
    alow[1] = updated.astype(jnp.bfloat16)
    loop(n, lambda d: a_copy(d, me).start(), far_first)
    phi[...] = jnp.zeros_like(phi)
    loop(n, lambda d: phi_copy(0, d, me).wait_send())
    aown[...] = updated
    al[1, me] = alow[1]
    loop(n, lambda d: a_copy(d, source(d)).wait_recv())
    spread(1)
    accumulate(False)
    total, _ = scattered(1)
    out[...] = aown[...] * total / mass

    when_carrier(lambda: loop(n_ka, lambda d: b_copy(d, ka).wait_send()))
    loop(n_ia, lambda d: c_copy(d, ia).wait_send())
    if paired:
        when_carrier(lambda: loop(n_ka, lambda d: b_hand(d).wait_send()))
    loop(n, lambda d: a_first(d).wait_send())
    loop(n, lambda d: a_copy(d, me).wait_send())
    loop(n, lambda d: phi_copy(1, d, me).wait_send())


def local(n_ia, n_ja, n_ka, block_coords, live_blocks, counts, factor_a, factor_b, factor_c):
    slots = block_coords.shape[-2]
    bs, cells = counts.shape[-2:]
    owned, rank = factor_a.shape
    rb = factor_b.shape[0]
    rc, wc = factor_c.shape
    n = n_ja * n_ka
    f32, bf16 = jnp.float32, jnp.bfloat16
    hbm = pl.BlockSpec(memory_space=pl.ANY)
    dma = pltpu.SemaphoreType.DMA
    return pl.pallas_call(
        functools.partial(kernel, n_ia, n_ja, n_ka, bs),
        out_shape=pltpu.VMEM((owned, rank), f32),
        in_specs=[hbm] * 6,
        out_specs=pl.BlockSpec(memory_space=pltpu.VMEM),
        scratch_shapes=[
            pltpu.SMEM((3, 1, slots), jnp.int32),
            pltpu.SMEM((1,), jnp.int32),
            pltpu.VMEM((slots, bs, cells), jnp.int32),
            pltpu.VMEM((rb, rank), f32),
            pltpu.VMEM((wc, rc), f32),
            pltpu.VMEM((rb, rank // 2), jnp.int32),
            pltpu.VMEM((wc, rc // 2), jnp.int32),
            pltpu.VMEM((n_ka * rb, rank // 2), jnp.int32),
            pltpu.VMEM((n_ia * wc, rc // 2), jnp.int32),
            pltpu.VMEM((n_ka * rb // bs, bs, rank), f32),
            pltpu.VMEM((rc // bs, bs, rank), f32),
            pltpu.VMEM((owned, rank), f32),
            pltpu.VMEM((2, owned, rank), bf16),
            pltpu.VMEM((2, n, owned, rank), bf16),
            pltpu.VMEM((RB1, bs, rank), bf16),
            pltpu.VMEM((slots, cells, rank), bf16),
            pltpu.VMEM((slots, rank, cells), bf16),
            pltpu.VMEM((RB1 * bs, rank), f32),
            pltpu.VMEM((n, owned + 2, rank // 2), jnp.int32),
            pltpu.VMEM((2, n, owned + 2, rank // 2), jnp.int32),
            pltpu.VMEM((RB1, 1, rank), f32),
            dma((6,)),
            dma((2, n_ka)),
            dma((2, n_ka)),
            dma((n_ia,)),
            dma((n_ia,)),
            dma((5, n)),
            dma((5, n)),
        ],
        compiler_params=pltpu.CompilerParams(
            collective_id=0, has_side_effects=True, vmem_limit_bytes=56 * 1024 * 1024
        ),
    )(
        jnp.swapaxes(block_coords, 3, 4).reshape(3, 1, slots), live_blocks.reshape(1),
        counts.reshape(slots, bs, cells), factor_a, factor_b, factor_c.T,
    )


def solution(mesh):
    placed = (
        P("ia", "ja", "ka", None, None),
        P("ia", "ja", "ka"),
        P("ia", "ja", "ka", None, None, None),
        P(("ia", "ja", "ka"), None),
        P(("ja", "ka"), None),
        P("ka", "ia"),
    )
    body = functools.partial(local, mesh.shape["ia"], mesh.shape["ja"], mesh.shape["ka"])
    return jax.shard_map(
        body, mesh=mesh, in_specs=placed, out_specs=P(("ia", "ja", "ka"), None), check_vma=False
    )
```
